256 devices in a mesh: fsdp: 16 (over y, x), tp: 8 (over z_hi, core), tower: 2 (over z_lo).
Axes of the slice: x: 4, y: 4, z: 8 (z_hi: 4, z_lo: 2; z = z_hi * 2 + z_lo), core: 2. Of those that a mesh axis runs over, the one named last changes fastest.
Arguments:
- images: bfloat16 [16384, 5120], P(('fsdp', 'tower')), may hold values from -61 to 61
- img_weight: bfloat16 [5120, 1024], P('fsdp', 'tp')
- texts: bfloat16 [16384, 1024], P(('fsdp', 'tp', 'tower')), may hold values from -1 to 1
- pair_perm: int32 [16384], P(('fsdp', 'tower')), may hold values from 0 to 16383, as said below
- forget: int32 [16384], P(('fsdp', 'tower')), may hold values 0 or 1
Outputs:
- pair_loss: float32 [16384], P(('fsdp', 'tower'))
- weight_grad: float32 [5120, 1024], P('fsdp', 'tp')
The draws below stay inside these ranges and needn't reach their ends.
Inputs may be any that keep to these rules, and one draw needn't show every extreme that they name: `pair_perm`: each number 0 to 16383 appears once.
All inputs are finite; a program needn't handle non-finite values. No bound on the sum of `forget` on one device may be relied on, other than what follows from the above.
Results may differ from the reference program's by a relative error of at most 0.0036.
Values may be sent and summed in bfloat16 or wider, within the bound.
No kernel may reach another device: no remote copies, remote signals or barrier semaphores. Data moves between devices by JAX's collectives and lax.ppermute only.
A program may use at most 64 MiB of HBM per device.

```python
import math
import jax
import jax.numpy as jnp
from jax import lax

IMAGE_WIDTH = 5120
EMBED = 1024
PAIRS = 16384


def base_images(key):
    images = jnp.clip(jax.random.normal(jax.random.fold_in(key, 11), (PAIRS, IMAGE_WIDTH), jnp.float32), -6.0, 6.0)
    return images.astype(jnp.bfloat16)


def base_weight(key):
    weight = jnp.clip(jax.random.normal(jax.random.fold_in(key, 13), (IMAGE_WIDTH, EMBED), jnp.float32), -5.0, 5.0)
    weight = weight * IMAGE_WIDTH ** (-0.5)
    return weight.astype(jnp.bfloat16)


def base_perm(key):
    return jax.random.permutation(jax.random.fold_in(key, 14), PAIRS).astype(jnp.int32)


def draw_images(key, part):
    return base_images(key)


def draw_img_weight(key, part):
    return base_weight(key)


def draw_pair_perm(key, part):
    return base_perm(key)


def draw_texts(key, part):
    texts = jax.random.normal(jax.random.fold_in(key, 15), (PAIRS, EMBED), jnp.float32) * EMBED ** (-0.5)
    texts = jnp.clip(texts, -0.25, 0.25)
    return jnp.clip(texts, -1.0, 1.0).astype(jnp.bfloat16)


def place_ends(values, rng, least, high):
    extent = values.shape
    place = [jax.random.randint(jax.random.fold_in(rng, axis), (), 0, extent[axis]) for axis in range(len(extent))]
    values = values.at[tuple(place)].set(least)
    longest = extent.index(max(extent))
    place[longest] = (place[longest] + 1) % extent[longest]
    return values.at[tuple(place)].set(high)


def setup_inputs(seed: int = 0) -> dict:
    key_list = jax.random.split(jax.random.key(seed), 6)
    images = draw_images(jax.random.fold_in(key_list[5], 71), 0)
    img_weight = draw_img_weight(jax.random.fold_in(key_list[5], 71), 0)
    texts = draw_texts(jax.random.fold_in(key_list[5], 71), 0)
    pair_perm = draw_pair_perm(jax.random.fold_in(key_list[5], 71), 0)
    forget = place_ends((jax.random.randint(key_list[4], (PAIRS,), 0, 4) < 1).astype(jnp.int32), jax.random.fold_in(key_list[4], 1), 0, 1)
    return dict(images=images, img_weight=img_weight, texts=texts, pair_perm=pair_perm, forget=forget)


epsilon = 1e-06
score_scale = 100.0

def reference(images, img_weight, texts, pair_perm, forget):
    emb = jnp.dot(images, img_weight, preferred_element_type=jnp.float32).astype(jnp.bfloat16)
    efloat = emb.astype(jnp.float32)
    rnorm = lax.rsqrt(lax.optimization_barrier(jnp.sum(efloat * efloat, axis=1, keepdims=True)) + epsilon)
    unit = efloat * rnorm
    unit_b = unit.astype(jnp.bfloat16)
    signs = 1.0 - 2.0 * forget.astype(jnp.float32)
    block = math.gcd(PAIRS, 512)
    nblocks = PAIRS // block
    columns = jnp.arange(PAIRS, dtype=jnp.int32)

    def one_block(args):
        unit_rows, perm_rows, sign_rows = args
        logits = score_scale * lax.dot_general(unit_rows, texts, (((1,), (1,)), ((), ())), preferred_element_type=jnp.float32)
        top = lax.optimization_barrier(jnp.max(logits, axis=1, keepdims=True))
        lse = top + jnp.log(lax.optimization_barrier(jnp.sum(jnp.exp(logits - top), axis=1, keepdims=True)))
        hit = perm_rows[:, None] == columns[None, :]
        positive = lax.optimization_barrier(jnp.sum(jnp.where(hit, logits, 0.0), axis=1))
        loss = lse[:, 0] - positive
        weights = (sign_rows[:, None] * (jnp.exp(logits - lse) - hit.astype(jnp.float32))).astype(jnp.bfloat16)
        grad_unit = score_scale * jnp.dot(weights, texts, preferred_element_type=jnp.float32)
        return (loss, grad_unit)
    loss, grad_unit = lax.map(one_block, (unit_b.reshape(nblocks, block, EMBED), pair_perm.reshape(nblocks, block), signs.reshape(nblocks, block)))
    loss = loss.reshape(PAIRS)
    grad_unit = grad_unit.reshape(PAIRS, EMBED)
    radial = lax.optimization_barrier(jnp.sum(unit * grad_unit, axis=1, keepdims=True))
    grad_emb = (rnorm * (grad_unit - unit * radial)).astype(jnp.bfloat16)
    weight_grad = lax.dot_general(images, grad_emb, (((0,), (0,)), ((), ())), preferred_element_type=jnp.float32)
    return (loss, weight_grad)
```

```python
import jax
import jax.numpy as jnp
from jax import lax
from jax.experimental import pallas as pl
from jax.experimental.pallas import tpu as pltpu
from jax.sharding import Mesh
from jax.sharding import PartitionSpec as P

AXES = ("y", "x", "zh", "core", "tw")
PLANE = ("y", "x")
FSDP_TOWER = ("y", "x", "tw")
REL = (0, 3, 1, 2)

epsilon = 1e-06
score_scale = 100.0
f32 = jnp.float32
bf16 = jnp.bfloat16
VMEM = pl.BlockSpec(memory_space=pltpu.VMEM)
HBM = pl.BlockSpec(memory_space=pltpu.HBM)
SMEM = pl.BlockSpec(memory_space=pltpu.SMEM)


def shifted(x, axis, step):
    n = lax.axis_size(axis)
    return lax.ppermute(x, axis, [(i, (i + step) % n) for i in range(n)])


def in_hbm(x):
    return pltpu.with_memory_space_constraint(x, pltpu.HBM)


def exchanged(x, axis):
    return lax.all_to_all(x, axis, 0, 0, tiled=True)


def from_all(x, axis):
    return exchanged(jnp.broadcast_to(x, (lax.axis_size(axis), *x.shape)), axis)


def gathered_texts(texts, other_texts):
    pieces = []
    for part, inner, outer in ((texts, "x", "y"), (other_texts, "y", "x")):
        below, above, far = (shifted(part, inner, step) for step in (1, -1, 2))
        halves = [jnp.concatenate([part, below]), jnp.concatenate([above, far])]
        for half, toward in zip(halves, (1, -1)):
            first = shifted(half, outer, toward)
            second = shifted(half, outer, -toward)
            far = shifted(first, outer, toward)
            pieces += [half, first, second, far] if toward == 1 else [half, second, first, far]
    return [in_hbm(piece) for piece in pieces]


def fetch(pieces, whole, sem):
    at, copies = 0, []
    for k, piece in enumerate(pieces):
        n = piece.shape[0]
        copies.append(pltpu.make_async_copy(piece, whole.at[pl.ds(at, n)], sem.at[k]))
        at += n
    for copy in copies:
        copy.start()
    return copies


def column_places(at_ref, group):
    y, x, tp, tower = (at_ref[k] for k in range(4))
    lane = lax.broadcasted_iota(jnp.int32, (1, 128), 1)
    places = []
    for side in range(2):
        tw = tower if side == 0 else 1 - tower
        for half in range(2):
            for step in REL:
                firsts = []
                for inner in REL[2 * half : 2 * half + 2]:
                    ahead = (step, inner) if side == 0 else (inner, step)
                    plane = lax.rem(y + ahead[0], 4) * 4 + lax.rem(x + ahead[1], 4)
                    firsts.append(((plane * 8 + tp) * 2 + tw) * group)
                places.append(jnp.where(lane < group, firsts[0], firsts[1] - group) + lane)
    return places


def as_columns(lines):
    n = lines[0].shape[1]
    spare = jnp.zeros((128 - len(lines), n), f32)
    return jnp.concatenate([*lines, spare], axis=0).T


def embed_kernel(images_ref, weight_ref, out_ref, total):
    k = pl.program_id(0)

    @pl.when(k == 0)
    def _():
        total[...] = jnp.zeros_like(total)

    total[...] += jnp.dot(images_ref[...], weight_ref[...], preferred_element_type=f32)

    @pl.when(k == pl.num_programs(0) - 1)
    def _():
        rounded = total[...].astype(bf16)
        for z in range(out_ref.shape[0]):
            out_ref[z] = rounded


def score_kernel(n_pieces, group, *refs):
    at_ref, mine_ref, theirs_ref, perm_ref = refs[:4]
    pieces = refs[4 : 4 + n_pieces]
    out_ref, stats_ref = refs[4 + n_pieces : 6 + n_pieces]
    whole, unit, score, high, soft, sem, out_sem = refs[6 + n_pieces :]
    copies = fetch(pieces, whole, sem)
    rows, feats = mine_ref.shape[1], mine_ref.shape[2]
    core = lax.rem(at_ref[2], 2)

    square = jnp.zeros((rows, feats), f32)
    for k in range(4):
        for ref in (mine_ref, theirs_ref):
            part = ref[k].astype(f32)
            square += part * part
    rnorm = lax.rsqrt(jnp.sum(square, axis=1, keepdims=True) + epsilon)
    for k in range(4):
        for ref, which in ((mine_ref, core), (theirs_ref, 1 - core)):
            to = pl.multiple_of((2 * k + which) * feats, feats)
            unit[:, pl.ds(to, feats)] = (ref[k].astype(f32) * rnorm).astype(bf16)
    high[...] = jnp.full_like(high, -jnp.inf)

    for copy in copies:
        copy.wait()
    step = 256

    @pl.loop(0, whole.shape[0] // step)
    def _(c):
        at = pl.multiple_of(c * step, step)
        chunk = score_scale * lax.dot_general(
            unit[...], whole[pl.ds(at, step)], (((1,), (1,)), ((), ())), preferred_element_type=f32
        )
        score[:, pl.ds(at, step)] = chunk
        high[...] = jnp.maximum(high[...], jnp.maximum(chunk[:, :128], chunk[:, 128:]))

    places = column_places(at_ref, group)
    band = 64

    @pl.loop(0, rows // band)
    def _(r):
        here = pl.ds(pl.multiple_of(r * band, band), band)
        perm = perm_ref[here, :]
        top = jnp.max(high[here, :], axis=1, keepdims=True)
        total = jnp.zeros((band, 128), f32)
        moment = jnp.zeros((band, 128), f32)
        found = jnp.zeros((band, 128), f32)
        for k in range(len(places)):
            cols = pl.ds(k * 128, 128)
            logit = score[here, cols]
            p = jnp.exp(logit - top)
            hit = perm == places[k]
            total += p
            moment += p * logit
            found += jnp.where(hit, logit, 0.0)
            soft[here, cols] = jnp.where(hit, 0.0, p).astype(bf16)
        pltpu.make_async_copy(soft.at[here], out_ref.at[here], out_sem).start()
        sums = [jnp.sum(v, axis=1, keepdims=True) for v in (total, moment, found)]
        which = lax.broadcasted_iota(jnp.int32, (band, 128), 1)
        tile = jnp.where(which == 0, top, 0.0)
        for k, v in enumerate(sums):
            tile = jnp.where(which == k + 1, v, tile)
        high[here, :] = tile

    which = lax.broadcasted_iota(jnp.int32, (rows, 128), 1)
    lines = jnp.where(which == 4, rnorm, high[...]).T
    stats_ref[...] = lines[:8]
    pltpu.make_async_copy(soft, out_ref, out_sem).wait()


def gradient_kernel(n_pieces, group, *refs):
    at_ref, perm_ref, p_ref = refs[:3]
    pieces = refs[3 : 3 + n_pieces]
    soft_ref, hard_ref = refs[3 + n_pieces : 5 + n_pieces]
    whole, both, sem, p_sem = refs[5 + n_pieces :]
    rows = soft_ref.shape[0]
    copies = [pltpu.make_async_copy(p_ref, both.at[pl.ds(0, rows)], p_sem)]
    copies[0].start()
    copies += fetch(pieces, whole, sem)
    places = column_places(at_ref, group)
    band = 64

    @pl.loop(0, rows // band)
    def _(r):
        at = pl.multiple_of(r * band, band)
        perm = perm_ref[pl.ds(at, band), :]
        for k in range(len(places)):
            both[pl.ds(at + rows, band), pl.ds(k * 128, 128)] = jnp.where(
                perm == places[k], 1.0, 0.0
            ).astype(bf16)

    for copy in copies:
        copy.wait()
    step = 256

    @pl.loop(0, whole.shape[1] // step)
    def _(c):
        cols = pl.ds(pl.multiple_of(c * step, step), step)
        out = jnp.dot(both[...], whole[:, cols], preferred_element_type=f32)
        soft_ref[:, cols] = out[:rows]
        hard_ref[:, cols] = out[rows:].astype(bf16)


def combine_kernel(at_ref, own_ref, every_ref, sign_ref, soft_ref, hard_ref, keep_ref, give_ref, lines_ref):
    core = lax.rem(at_ref[2], 2)
    feats = keep_ref.shape[2]
    rest = [every_ref[k] for k in range(every_ref.shape[0])]
    tops = [v[0:1] for v in rest]
    high = tops[0]
    for t in tops[1:]:
        high = jnp.maximum(high, t)
    scales = [jnp.exp(t - high) for t in tops]
    mass = sum(s * v[1:2] for s, v in zip(scales, rest))
    lse = high + jnp.log(mass)
    target = sum(v[3:4] for v in rest)
    mean = sum(jnp.exp(t - lse) * v[2:3] for t, v in zip(tops, rest))
    sign = sign_ref[...]
    lines_ref[0:1] = lse - target
    lines_ref[1:2] = sign * (mean - target)
    lines_ref[2:3] = own_ref[4:5]
    for_soft = score_scale * sign * jnp.exp(own_ref[0:1] - lse)
    weight = (sign * (jnp.exp(target - lse) - 1.0)).astype(bf16).astype(f32)
    cols = as_columns([for_soft, score_scale * weight])
    first, second = cols[:, 0:1], cols[:, 1:2]
    for k in range(4):
        for out, which in ((keep_ref, core), (give_ref, 1 - core)):
            at = pl.ds(pl.multiple_of((2 * k + which) * feats, feats), feats)
            out[k] = first * soft_ref[:, at] + second * hard_ref[:, at].astype(f32)


def local(images, img_weight, texts, pair_perm, forget):
    y, x, zh = (lax.axis_index(a) for a in ("y", "x", "zh"))
    core, tower = lax.axis_index("core"), lax.axis_index("tw")
    rows, width = images.shape
    feats = img_weight.shape[1]
    group = texts.shape[0]
    at = jnp.stack([y, x, zh * 2 + core, tower]).astype(jnp.int32)
    signs = 1.0 - 2.0 * forget.astype(f32)
    perm = pair_perm.reshape(rows, 1)

    weight = from_all(img_weight, PLANE).reshape(width, feats)
    other_texts = shifted(texts, "tw", 1)
    pieces = gathered_texts(texts, other_texts)
    n = len(pieces)
    texts_here = sum(piece.shape[0] for piece in pieces)
    embed = pieces[0].shape[1]

    block = 640
    emb_copies = pl.pallas_call(
        embed_kernel,
        name="embed",
        grid=(width // block,),
        out_shape=jax.ShapeDtypeStruct((4, rows, feats), bf16),
        in_specs=[
            pl.BlockSpec((rows, block), lambda k: (0, k)),
            pl.BlockSpec((block, feats), lambda k: (k, 0)),
        ],
        out_specs=pl.BlockSpec((4, rows, feats), lambda k: (0, 0, 0)),
        scratch_shapes=[pltpu.VMEM((rows, feats), f32)],
        compiler_params=pltpu.CompilerParams(vmem_limit_bytes=8 << 20),
        cost_estimate=pl.CostEstimate(
            flops=2 * rows * width * feats, bytes_accessed=7 << 20, transcendentals=0
        ),
    )(in_hbm(images), weight)
    emb_part = emb_copies[0]
    mine = exchanged(emb_copies, "zh")
    theirs = shifted(mine, "core", 1)

    p, stats = pl.pallas_call(
        lambda *refs: score_kernel(n, group, *refs),
        name="scores",
        out_shape=(
            pltpu.HBM((rows, texts_here), bf16),
            jax.ShapeDtypeStruct((8, rows), f32),
        ),
        in_specs=[SMEM, VMEM, VMEM, VMEM, *[HBM] * n],
        out_specs=(HBM, VMEM),
        scratch_shapes=[
            pltpu.VMEM((texts_here, embed), bf16),
            pltpu.VMEM((rows, embed), bf16),
            pltpu.VMEM((rows, texts_here), f32),
            pltpu.VMEM((rows, 128), f32),
            pltpu.VMEM((rows, texts_here), bf16),
            pltpu.SemaphoreType.DMA((n,)),
            pltpu.SemaphoreType.DMA,
        ],
        compiler_params=pltpu.CompilerParams(vmem_limit_bytes=20 << 20),
        cost_estimate=pl.CostEstimate(
            flops=2 * rows * texts_here * embed,
            bytes_accessed=8 << 20,
            transcendentals=rows * texts_here,
        ),
    )(at, mine, theirs, perm, *pieces)

    every = from_all(stats, ("zh", "core"))

    soft, hard = pl.pallas_call(
        lambda *refs: gradient_kernel(n, group, *refs),
        name="gradient",
        out_shape=(
            jax.ShapeDtypeStruct((rows, embed), f32),
            jax.ShapeDtypeStruct((rows, embed), bf16),
        ),
        in_specs=[SMEM, VMEM, HBM, *[HBM] * n],
        out_specs=(VMEM, VMEM),
        scratch_shapes=[
            pltpu.VMEM((texts_here, embed), bf16),
            pltpu.VMEM((2 * rows, texts_here), bf16),
            pltpu.SemaphoreType.DMA((n,)),
            pltpu.SemaphoreType.DMA,
        ],
        compiler_params=pltpu.CompilerParams(vmem_limit_bytes=20 << 20),
        cost_estimate=pl.CostEstimate(
            flops=4 * rows * texts_here * embed, bytes_accessed=10 << 20, transcendentals=0
        ),
    )(at, perm, in_hbm(p), *pieces)

    keep, give, lines = pl.pallas_call(
        combine_kernel,
        name="combine",
        out_shape=(
            jax.ShapeDtypeStruct((4, rows, feats), f32),
            jax.ShapeDtypeStruct((4, rows, feats), f32),
            jax.ShapeDtypeStruct((8, rows), f32),
        ),
        in_specs=[SMEM, VMEM, VMEM, VMEM, VMEM, VMEM],
        out_specs=(VMEM, VMEM, VMEM),
        compiler_params=pltpu.CompilerParams(vmem_limit_bytes=20 << 20),
    )(at, stats, every, signs.reshape(1, rows), soft, hard)

    pair_loss, radial, rnorm = lines[0], lines[1], lines[2]
    chip = keep + shifted(give, "core", 1)
    parts = exchanged(chip.astype(bf16), "zh")
    mask = (jnp.arange(4) == zh)[:, None, None]
    grad_unit = jnp.sum(jnp.where(mask, chip, parts.astype(f32)), axis=0)
    unit_part = emb_part.astype(f32) * rnorm[:, None]
    grad_emb = (rnorm[:, None] * (grad_unit - unit_part * radial[:, None])).astype(bf16)
    share = lax.dot_general(
        images, grad_emb, (((0,), (0,)), ((), ())), preferred_element_type=f32
    ).astype(bf16)
    summed = jnp.sum(exchanged(share.reshape(16, -1, feats), PLANE).astype(f32), axis=0)
    weight_grad = summed + shifted(summed, "tw", 1)
    return (pair_loss, weight_grad)


def solution(mesh):
    finer = Mesh(mesh.devices.reshape(4, 4, 4, 2, mesh.shape["tower"]), AXES)
    return jax.shard_map(
        local,
        mesh=finer,
        in_specs=(
            P(FSDP_TOWER, None),
            P(PLANE, ("zh", "core")),
            P(("y", "x", "zh", "core", "tw"), None),
            P(FSDP_TOWER),
            P(FSDP_TOWER),
        ),
        out_specs=(P(FSDP_TOWER), P(PLANE, ("zh", "core"))),
        check_vma=False,
    )
```

```python
import jax
import jax.numpy as jnp
from jax import lax
from jax.experimental import pallas as pl
from jax.experimental.pallas import tpu as pltpu
from jax.sharding import Mesh
from jax.sharding import PartitionSpec as P

AXES = ("y", "x", "zh", "core", "tw")
PLANE = ("y", "x")
FSDP_TOWER = ("y", "x", "tw")
REL = (0, 3, 1, 2)
NEAR = (0, 3, 1)
FAR = (2,)

epsilon = 1e-06
score_scale = 100.0
f32 = jnp.float32
bf16 = jnp.bfloat16
VMEM = pl.BlockSpec(memory_space=pltpu.VMEM)
HBM = pl.BlockSpec(memory_space=pltpu.HBM)
SMEM = pl.BlockSpec(memory_space=pltpu.SMEM)


def shifted(x, axis, step):
    n = lax.axis_size(axis)
    return lax.ppermute(x, axis, [(i, (i + step) % n) for i in range(n)])


def in_hbm(x):
    return pltpu.with_memory_space_constraint(x, pltpu.HBM)


def exchanged(x, axis):
    return lax.all_to_all(x, axis, 0, 0, tiled=True)


def from_all(x, axis):
    return exchanged(jnp.broadcast_to(x, (lax.axis_size(axis), *x.shape)), axis)


def gathered_texts(texts, other_texts):
    near, far = [], []
    for part, inner, outer in ((texts, "x", "y"), (other_texts, "y", "x")):
        below, above, across = (shifted(part, inner, step) for step in (1, -1, 2))
        halves = [jnp.concatenate([part, below]), jnp.concatenate([above, across])]
        for half, toward in zip(halves, (1, -1)):
            first = shifted(half, outer, toward)
            second = shifted(half, outer, -toward)
            near += [half, first, second] if toward == 1 else [half, second, first]
            far.append(shifted(first, outer, toward))
    return [in_hbm(piece) for piece in near], [in_hbm(piece) for piece in far]


def fetch(pieces, whole, sem):
    at, copies = 0, []
    for k, piece in enumerate(pieces):
        n = piece.shape[0]
        copies.append(pltpu.make_async_copy(piece, whole.at[pl.ds(at, n)], sem.at[k]))
        at += n
    for copy in copies:
        copy.start()
    return copies


def column_places(at_ref, group, steps):
    y, x, tp, tower = (at_ref[k] for k in range(4))
    lane = lax.broadcasted_iota(jnp.int32, (1, 128), 1)
    places = []
    for side in range(2):
        tw = tower if side == 0 else 1 - tower
        for half in range(2):
            for step in steps:
                firsts = []
                for inner in REL[2 * half : 2 * half + 2]:
                    ahead = (step, inner) if side == 0 else (inner, step)
                    plane = lax.rem(y + ahead[0], 4) * 4 + lax.rem(x + ahead[1], 4)
                    firsts.append(((plane * 8 + tp) * 2 + tw) * group)
                places.append(jnp.where(lane < group, firsts[0], firsts[1] - group) + lane)
    return places


def as_columns(lines):
    n = lines[0].shape[1]
    spare = jnp.zeros((128 - len(lines), n), f32)
    return jnp.concatenate([*lines, spare], axis=0).T


def column_copies(whole, held, sem, step):
    copies = []
    for k in range(whole.shape[1] // step):
        here = pl.ds(k * step, step)
        copies.append(pltpu.make_async_copy(whole.at[:, here], held.at[:, here], sem.at[k]))
        copies[-1].start()
    return copies


def gate_kernel(in_ref, out_ref):
    out_ref[...] = in_ref[...]


def sign_kernel(forget_ref, out_ref):
    out_ref[...] = 1.0 - 2.0 * forget_ref[...].astype(f32)


def place_kernel(perm_ref, out_ref):
    out_ref[...] = as_columns([perm_ref[...].astype(f32)])[:, 0:1].astype(jnp.int32)


def embed_kernel(images_ref, weight_ref, out_ref, held, sem):
    step = 128
    copies = []
    for k in range(images_ref.shape[0] // step):
        here = pl.ds(k * step, step)
        copies.append(pltpu.make_async_copy(images_ref.at[here], held.at[here], sem.at[k]))
        copies[-1].start()
    for k, copy in enumerate(copies):
        copy.wait()
        here = pl.ds(k * step, step)
        rounded = jnp.dot(
            held[here, :], weight_ref[...], preferred_element_type=f32
        ).astype(bf16)
        for z in range(out_ref.shape[0]):
            out_ref[z, here, :] = rounded


def merged(one, two):
    top = jnp.maximum(one[0:1], two[0:1])
    first, second = jnp.exp(one[0:1] - top), jnp.exp(two[0:1] - top)
    total = one[1:2] * first + two[1:2] * second
    moment = one[2:3] * first + two[2:3] * second
    return jnp.concatenate([top, total, moment, one[3:4] + two[3:4], one[4:8]], axis=0)


def score_columns(unit, pieces, whole, score, high, soft, sem, out_sem, at_ref, perm_ref, out_ref, group, steps, rnorm):
    copies = fetch(pieces, whole, sem)
    rows = unit.shape[0]
    step = 512
    per = step // pieces[0].shape[0]
    for c in range(whole.shape[0] // step):
        for copy in copies[c * per : (c + 1) * per]:
            copy.wait()
        at = c * step
        chunk = score_scale * lax.dot_general(
            unit[...], whole[pl.ds(at, step)], (((1,), (1,)), ((), ())), preferred_element_type=f32
        )
        score[:, pl.ds(at, step)] = chunk
        peak = chunk[:, :128]
        for k in range(128, step, 128):
            peak = jnp.maximum(peak, chunk[:, k : k + 128])
        high[...] = peak if c == 0 else jnp.maximum(high[...], peak)

    places = column_places(at_ref, group, steps)
    band = 128

    @pl.loop(0, rows // band)
    def _(r):
        here = pl.ds(pl.multiple_of(r * band, band), band)
        perm = perm_ref[here, :]
        top = jnp.max(high[here, :], axis=1, keepdims=True)
        total = jnp.zeros((band, 128), f32)
        moment = jnp.zeros((band, 128), f32)
        found = jnp.zeros((band, 128), f32)
        for k in range(len(places)):
            cols = pl.ds(k * 128, 128)
            logit = score[here, cols]
            p = jnp.exp(logit - top)
            hit = perm == places[k]
            total += p
            moment += p * logit
            found += jnp.where(hit, logit, 0.0)
            soft[here, cols] = jnp.where(hit, 0.0, p).astype(bf16)
        pltpu.make_async_copy(soft.at[here], out_ref.at[here], out_sem).start()
        sums = [jnp.sum(v, axis=1, keepdims=True) for v in (total, moment, found)]
        which = lax.broadcasted_iota(jnp.int32, (band, 128), 1)
        tile = jnp.where(which == 0, top, 0.0)
        for k, v in enumerate(sums):
            tile = jnp.where(which == k + 1, v, tile)
        high[here, :] = tile

    filled = high[...]
    if rnorm is not None:
        which = lax.broadcasted_iota(jnp.int32, (rows, 128), 1)
        filled = jnp.where(which == 4, rnorm, filled)
    lines = filled.T[:8]
    pltpu.make_async_copy(soft, out_ref, out_sem).wait()
    return lines


def near_score_kernel(n, group, *refs):
    at_ref, mine_ref, theirs_ref, perm_ref = refs[:4]
    pieces = refs[4 : 4 + n]
    out_ref, stats_ref, unit = refs[4 + n : 7 + n]
    whole, score, high, soft, sem, out_sem = refs[7 + n :]
    rows, feats = mine_ref.shape[1], mine_ref.shape[2]
    core = lax.rem(at_ref[2], 2)
    square = jnp.zeros((rows, feats), f32)
    for k in range(4):
        for ref in (mine_ref, theirs_ref):
            part = ref[k].astype(f32)
            square += part * part
    rnorm = lax.rsqrt(jnp.sum(square, axis=1, keepdims=True) + epsilon)
    for k in range(4):
        for ref, which in ((mine_ref, core), (theirs_ref, 1 - core)):
            to = pl.multiple_of((2 * k + which) * feats, feats)
            unit[:, pl.ds(to, feats)] = (ref[k].astype(f32) * rnorm).astype(bf16)
    stats_ref[...] = score_columns(
        unit, pieces, whole, score, high, soft, sem, out_sem, at_ref, perm_ref, out_ref, group, NEAR, rnorm
    )


def far_score_kernel(n, group, *refs):
    at_ref, unit, perm_ref, near_ref = refs[:4]
    pieces = refs[4 : 4 + n]
    out_ref, stats_ref, every_ref = refs[4 + n : 7 + n]
    whole, score, high, soft, sem, out_sem = refs[7 + n :]
    lines = score_columns(
        unit, pieces, whole, score, high, soft, sem, out_sem, at_ref, perm_ref, out_ref, group, FAR, None
    )
    stats_ref[...] = lines
    both = merged(near_ref[...], lines)
    for k in range(every_ref.shape[0]):
        every_ref[k] = both


def gradient_columns(at_ref, perm_ref, p_ref, pieces, whole, both, sem, p_sem, group, steps):
    rows = p_ref.shape[0]
    p_copy = pltpu.make_async_copy(p_ref, both.at[pl.ds(0, rows)], p_sem)
    p_copy.start()
    step = 512
    for c in range(whole.shape[1] // step):
        cols, at = pl.ds(c * step, step), 0
        for piece in pieces:
            there = whole.at[pl.ds(at, piece.shape[0]), cols]
            pltpu.make_async_copy(piece.at[:, cols], there, sem.at[c]).start()
            at += piece.shape[0]
    places = column_places(at_ref, group, steps)
    band = 64

    @pl.loop(0, rows // band)
    def _(r):
        at = pl.multiple_of(r * band, band)
        perm = perm_ref[pl.ds(at, band), :]
        for k in range(len(places)):
            both[pl.ds(at + rows, band), pl.ds(k * 128, 128)] = jnp.where(
                perm == places[k], 1.0, 0.0
            ).astype(bf16)

    p_copy.wait()
    for c in range(whole.shape[1] // step):
        cols = pl.ds(c * step, step)
        pltpu.make_async_copy(whole.at[:, cols], whole.at[:, cols], sem.at[c]).wait()
        out = jnp.dot(both[...], whole[:, cols], preferred_element_type=f32)
        yield cols, out[:rows], out[rows:]


def near_gradient_kernel(n, group, *refs):
    at_ref, perm_ref, p_ref = refs[:3]
    pieces = refs[3 : 3 + n]
    soft_ref, hard_ref = refs[3 + n : 5 + n]
    for cols, soft, hard in gradient_columns(
        at_ref, perm_ref, p_ref, pieces, *refs[5 + n :], group, NEAR
    ):
        soft_ref[:, cols] = soft
        hard_ref[:, cols] = hard.astype(bf16)


def far_gradient_kernel(n, group, *refs):
    at_ref, perm_ref, p_ref, near_ref, far_ref, near_soft, near_hard = refs[:7]
    pieces = refs[7 : 7 + n]
    soft_ref, hard_ref = refs[7 + n : 9 + n]
    top = jnp.maximum(near_ref[0:1], far_ref[0:1])
    cols = as_columns([jnp.exp(near_ref[0:1] - top), jnp.exp(far_ref[0:1] - top)])
    first, second = cols[:, 0:1], cols[:, 1:2]
    for cols, soft, hard in gradient_columns(
        at_ref, perm_ref, p_ref, pieces, *refs[9 + n :], group, FAR
    ):
        soft_ref[:, cols] = first * near_soft[:, cols] + second * soft
        hard_ref[:, cols] = near_hard[:, cols] + hard.astype(bf16)


def combine_kernel(at_ref, near_ref, far_ref, every_ref, sign_ref, soft_ref, hard_ref, keep_ref, give_ref, lines_ref):
    core = lax.rem(at_ref[2], 2)
    feats = keep_ref.shape[2]
    rest = [every_ref[k] for k in range(every_ref.shape[0])]
    tops = [v[0:1] for v in rest]
    high = tops[0]
    for t in tops[1:]:
        high = jnp.maximum(high, t)
    scales = [jnp.exp(t - high) for t in tops]
    mass = sum(s * v[1:2] for s, v in zip(scales, rest))
    lse = high + jnp.log(mass)
    target = sum(v[3:4] for v in rest)
    mean = sum(jnp.exp(t - lse) * v[2:3] for t, v in zip(tops, rest))
    sign = sign_ref[...]
    lines_ref[0:1] = lse - target
    lines_ref[1:2] = sign * (mean - target)
    lines_ref[2:3] = near_ref[4:5]
    for_soft = score_scale * sign * jnp.exp(jnp.maximum(near_ref[0:1], far_ref[0:1]) - lse)
    weight = (sign * (jnp.exp(target - lse) - 1.0)).astype(bf16).astype(f32)
    cols = as_columns([for_soft, score_scale * weight])
    first, second = cols[:, 0:1], cols[:, 1:2]
    for k in range(4):
        for out, which in ((keep_ref, core), (give_ref, 1 - core)):
            at = pl.ds(pl.multiple_of((2 * k + which) * feats, feats), feats)
            out[k] = first * soft_ref[:, at] + second * hard_ref[:, at].astype(f32)


def weight_kernel(at_ref, images_ref, chip_ref, parts_ref, emb_ref, lines_ref, out_ref, held, sem):
    step = 1024
    copies = column_copies(images_ref, held, sem, step)
    zh = lax.div(at_ref[2], 2)
    grad_unit = jnp.zeros(chip_ref.shape[1:], f32)
    for k in range(4):
        grad_unit += jnp.where(zh == k, chip_ref[k], parts_ref[k].astype(f32))
    cols = as_columns([lines_ref[1:2], lines_ref[2:3]])
    radial, rnorm = cols[:, 0:1], cols[:, 1:2]
    unit = emb_ref[0].astype(f32) * rnorm
    grad_emb = (rnorm * (grad_unit - unit * radial)).astype(bf16)
    for k, copy in enumerate(copies):
        copy.wait()
        here = pl.ds(k * step, step)
        out_ref[here, :] = lax.dot_general(
            held[:, here], grad_emb, (((0,), (0,)), ((), ())), preferred_element_type=f32
        ).astype(bf16)


def local(images, img_weight, texts, pair_perm, forget):
    y, x, zh = (lax.axis_index(a) for a in ("y", "x", "zh"))
    core, tower = lax.axis_index("core"), lax.axis_index("tw")
    rows, width = images.shape
    feats = img_weight.shape[1]
    group = texts.shape[0]
    at = jnp.stack([y, x, zh * 2 + core, tower]).astype(jnp.int32)

    weight = from_all(img_weight, PLANE).reshape(width, feats)
    other_texts = shifted(texts, "tw", 1)
    other_texts = pl.pallas_call(
        gate_kernel,
        name="gate",
        out_shape=jax.ShapeDtypeStruct(texts.shape, bf16),
        in_specs=[VMEM],
        out_specs=VMEM,
        compiler_params=pltpu.CompilerParams(vmem_limit_bytes=2 << 20),
    )(other_texts)
    signs = pl.pallas_call(
        sign_kernel,
        name="signs",
        out_shape=jax.ShapeDtypeStruct((1, rows), f32),
        in_specs=[VMEM],
        out_specs=VMEM,
        compiler_params=pltpu.CompilerParams(vmem_limit_bytes=2 << 20),
    )(forget.reshape(1, rows))
    perm = pl.pallas_call(
        place_kernel,
        name="places",
        out_shape=jax.ShapeDtypeStruct((rows, 1), jnp.int32),
        in_specs=[VMEM],
        out_specs=VMEM,
        compiler_params=pltpu.CompilerParams(vmem_limit_bytes=2 << 20),
    )(pair_perm.reshape(1, rows))
    near, far = gathered_texts(texts, other_texts)
    n, m = len(near), len(far)
    near_rows, far_rows = (sum(q.shape[0] for q in group) for group in (near, far))
    embed = near[0].shape[1]

    emb_copies = pl.pallas_call(
        embed_kernel,
        name="embed",
        out_shape=jax.ShapeDtypeStruct((4, rows, feats), bf16),
        in_specs=[HBM, VMEM],
        out_specs=VMEM,
        scratch_shapes=[pltpu.VMEM((rows, width), bf16), pltpu.SemaphoreType.DMA((rows // 128,))],
        compiler_params=pltpu.CompilerParams(vmem_limit_bytes=16 << 20),
        cost_estimate=pl.CostEstimate(
            flops=2 * rows * width * feats, bytes_accessed=7 << 20, transcendentals=0
        ),
    )(in_hbm(images), weight)
    mine = exchanged(emb_copies, "zh")
    theirs = shifted(mine, "core", 1)

    def score_scratch(count, columns):
        return [
            pltpu.VMEM((columns, embed), bf16),
            pltpu.VMEM((rows, columns), f32),
            pltpu.VMEM((rows, 128), f32),
            pltpu.VMEM((rows, columns), bf16),
            pltpu.SemaphoreType.DMA((count,)),
            pltpu.SemaphoreType.DMA,
        ]

    def gradient_scratch(columns):
        return [
            pltpu.VMEM((columns, embed), bf16),
            pltpu.VMEM((2 * rows, columns), bf16),
            pltpu.SemaphoreType.DMA((embed // 512,)),
            pltpu.SemaphoreType.DMA,
        ]

    def cost(flops, columns):
        return pl.CostEstimate(
            flops=flops, bytes_accessed=4 * embed * columns, transcendentals=rows * columns
        )

    gradient_shape = (
        jax.ShapeDtypeStruct((rows, embed), f32),
        jax.ShapeDtypeStruct((rows, embed), bf16),
    )
    work = 2 * rows * embed
    near_p, near_stats, unit = pl.pallas_call(
        lambda *refs: near_score_kernel(n, group, *refs),
        name="near_scores",
        out_shape=(
            pltpu.HBM((rows, near_rows), bf16),
            jax.ShapeDtypeStruct((8, rows), f32),
            jax.ShapeDtypeStruct((rows, embed), bf16),
        ),
        in_specs=[SMEM, VMEM, VMEM, VMEM, *[HBM] * n],
        out_specs=(HBM, VMEM, VMEM),
        scratch_shapes=score_scratch(n, near_rows),
        compiler_params=pltpu.CompilerParams(vmem_limit_bytes=20 << 20),
        cost_estimate=cost(work * near_rows, near_rows),
    )(at, mine, theirs, perm, *near)
    near_p = in_hbm(near_p)
    near_soft, near_hard = pl.pallas_call(
        lambda *refs: near_gradient_kernel(n, group, *refs),
        name="near_gradient",
        out_shape=gradient_shape,
        in_specs=[SMEM, VMEM, HBM, *[HBM] * n],
        out_specs=(VMEM, VMEM),
        scratch_shapes=gradient_scratch(near_rows),
        compiler_params=pltpu.CompilerParams(vmem_limit_bytes=20 << 20),
        cost_estimate=cost(2 * work * near_rows, near_rows),
    )(at, perm, near_p, *near)
    far_p, far_stats, copies = pl.pallas_call(
        lambda *refs: far_score_kernel(m, group, *refs),
        name="far_scores",
        out_shape=(
            pltpu.HBM((rows, far_rows), bf16),
            jax.ShapeDtypeStruct((8, rows), f32),
            jax.ShapeDtypeStruct((8, 8, rows), f32),
        ),
        in_specs=[SMEM, VMEM, VMEM, VMEM, *[HBM] * m],
        out_specs=(HBM, VMEM, VMEM),
        scratch_shapes=score_scratch(m, far_rows),
        compiler_params=pltpu.CompilerParams(vmem_limit_bytes=20 << 20),
        cost_estimate=cost(work * far_rows, far_rows),
    )(at, unit, perm, near_stats, *far)
    every = exchanged(copies, ("zh", "core"))
    soft, hard = pl.pallas_call(
        lambda *refs: far_gradient_kernel(m, group, *refs),
        name="far_gradient",
        out_shape=gradient_shape,
        in_specs=[SMEM, VMEM, HBM, VMEM, VMEM, VMEM, VMEM, *[HBM] * m],
        out_specs=(VMEM, VMEM),
        scratch_shapes=gradient_scratch(far_rows),
        compiler_params=pltpu.CompilerParams(vmem_limit_bytes=20 << 20),
        cost_estimate=cost(2 * work * far_rows, far_rows),
    )(at, perm, in_hbm(far_p), near_stats, far_stats, near_soft, near_hard, *far)

    keep, give, lines = pl.pallas_call(
        combine_kernel,
        name="combine",
        out_shape=(
            jax.ShapeDtypeStruct((4, rows, feats), f32),
            jax.ShapeDtypeStruct((4, rows, feats), f32),
            jax.ShapeDtypeStruct((8, rows), f32),
        ),
        in_specs=[SMEM, VMEM, VMEM, VMEM, VMEM, VMEM, VMEM],
        out_specs=(VMEM, VMEM, VMEM),
        compiler_params=pltpu.CompilerParams(vmem_limit_bytes=20 << 20),
    )(at, near_stats, far_stats, every, signs, soft, hard)

    pair_loss = lines[0]
    chip = keep + shifted(give, "core", 1)
    parts = exchanged(chip.astype(bf16), "zh")
    share = pl.pallas_call(
        weight_kernel,
        name="weight",
        out_shape=jax.ShapeDtypeStruct((width, feats), bf16),
        in_specs=[SMEM, HBM, VMEM, VMEM, VMEM, VMEM],
        out_specs=VMEM,
        scratch_shapes=[pltpu.VMEM((rows, width), bf16), pltpu.SemaphoreType.DMA((width // 1024,))],
        compiler_params=pltpu.CompilerParams(vmem_limit_bytes=16 << 20),
    )(at, in_hbm(images), chip, parts, emb_copies, lines)
    summed = jnp.sum(exchanged(share.reshape(16, -1, feats), PLANE).astype(f32), axis=0)
    weight_grad = summed + shifted(summed, "tw", 1)
    return (pair_loss, weight_grad)


def solution(mesh):
    finer = Mesh(mesh.devices.reshape(4, 4, 4, 2, mesh.shape["tower"]), AXES)
    return jax.shard_map(
        local,
        mesh=finer,
        in_specs=(
            P(FSDP_TOWER, None),
            P(PLANE, ("zh", "core")),
            P(("y", "x", "zh", "core", "tw"), None),
            P(FSDP_TOWER),
            P(FSDP_TOWER),
        ),
        out_specs=(P(FSDP_TOWER), P(PLANE, ("zh", "core"))),
        check_vma=False,
    )
```

```python
import jax
import jax.numpy as jnp
from jax import lax
from jax.experimental import pallas as pl
from jax.experimental.pallas import tpu as pltpu
from jax.sharding import Mesh
from jax.sharding import PartitionSpec as P

AXES = ("y", "x", "zh", "core", "tw")
PLANE = ("y", "x")
FSDP_TOWER = ("y", "x", "tw")
REL = (0, 3, 1, 2)
NEAR = (0, 3, 1)
AROUND = (0, 3, 1, 2)
FAR = (2,)

epsilon = 1e-06
score_scale = 100.0
f32 = jnp.float32
bf16 = jnp.bfloat16
VMEM = pl.BlockSpec(memory_space=pltpu.VMEM)
HBM = pl.BlockSpec(memory_space=pltpu.HBM)


def shifted(x, axis, step):
    n = lax.axis_size(axis)
    return lax.ppermute(x, axis, [(i, (i + step) % n) for i in range(n)])


def in_hbm(x):
    return pltpu.with_memory_space_constraint(x, pltpu.HBM)


def exchanged(x, axis):
    return lax.all_to_all(x, axis, 0, 0, tiled=True)


def from_others(x, axis):
    return [shifted(x, axis, step) for step in (1, -1, 2)]


def gathered_texts(texts, other_texts):
    near, far = [], []
    for part, inner, outer in ((texts, "x", "y"), (other_texts, "y", "x")):
        below, above, across = (shifted(part, inner, step) for step in (1, -1, 2))
        halves = [jnp.concatenate([part, below]), jnp.concatenate([above, across])]
        for half, toward in zip(halves, (1, -1)):
            first = shifted(half, outer, toward)
            second = shifted(half, outer, -toward)
            near += [half, first, second] if toward == 1 else [half, second, first]
            far.append(shifted(first, outer, toward))
    return [in_hbm(piece) for piece in near], [in_hbm(piece) for piece in far]


def fetch(pieces, whole, sem):
    at, copies = 0, []
    for k, piece in enumerate(pieces):
        n = piece.shape[0]
        copies.append(pltpu.make_async_copy(piece, whole.at[pl.ds(at, n)], sem.at[k]))
        at += n
    for copy in copies:
        copy.start()
    return copies


def tp_index():
    return lax.axis_index("zh") * 2 + lax.axis_index("core")


def column_places(group, steps):
    y, x, tp, tower = lax.axis_index("y"), lax.axis_index("x"), tp_index(), lax.axis_index("tw")
    lane = lax.broadcasted_iota(jnp.int32, (1, 128), 1)
    places = []
    for side in range(2):
        tw = tower if side == 0 else 1 - tower
        for half in range(2):
            for step in steps:
                firsts = []
                for inner in REL[2 * half : 2 * half + 2]:
                    ahead = (step, inner) if side == 0 else (inner, step)
                    plane = lax.rem(y + ahead[0], 4) * 4 + lax.rem(x + ahead[1], 4)
                    firsts.append(((plane * 8 + tp) * 2 + tw) * group)
                places.append(jnp.where(lane < group, firsts[0], firsts[1] - group) + lane)
    return places


def as_columns(lines):
    n = lines[0].shape[1]
    spare = jnp.zeros((128 - len(lines), n), f32)
    return jnp.concatenate([*lines, spare], axis=0).T


def column_copies(whole, held, sem, step):
    copies = []
    for k in range(whole.shape[1] // step):
        here = pl.ds(k * step, step)
        copies.append(pltpu.make_async_copy(whole.at[:, here], held.at[:, here], sem.at[k]))
        copies[-1].start()
    return copies


def gate_kernel(in_ref, out_ref):
    out_ref[...] = in_ref[...]


def spread_kernel(in_ref, out_ref, sem):
    copies = [pltpu.make_async_copy(in_ref, out_ref.at[k], sem.at[k]) for k in range(16)]
    for copy in copies:
        copy.start()
    for copy in copies:
        copy.wait()


def sign_kernel(forget_ref, out_ref, sign, sem):
    sign[...] = 1.0 - 2.0 * forget_ref[...].astype(f32)
    copy = pltpu.make_async_copy(sign, out_ref, sem)
    copy.start()
    copy.wait()


def place_kernel(perm_ref, out_ref):
    out_ref[...] = as_columns([perm_ref[...].astype(f32)])[:, 0:1].astype(jnp.int32)


def embed_kernel(images_ref, weight_ref, out_ref, held, rounded, sem, out_sem):
    step = 128
    for k in range(images_ref.shape[0] // step):
        here = pl.ds(k * step, step)
        pltpu.make_async_copy(images_ref.at[here], held.at[here], sem.at[k]).start()

    @pl.loop(0, images_ref.shape[0] // step)
    def _(k):
        here = pl.ds(pl.multiple_of(k * step, step), step)
        pltpu.make_async_copy(images_ref.at[here], held.at[here], sem.at[k]).wait()
        rounded[here, :] = jnp.dot(
            held[here, :], weight_ref[...], preferred_element_type=f32
        ).astype(bf16)
        pltpu.make_async_copy(rounded.at[here], out_ref.at[here], out_sem).start()

    pltpu.make_async_copy(rounded, out_ref, out_sem).wait()


def merged(one, two):
    top = jnp.maximum(one[0:1], two[0:1])
    first, second = jnp.exp(one[0:1] - top), jnp.exp(two[0:1] - top)
    total = one[1:2] * first + two[1:2] * second
    moment = one[2:3] * first + two[2:3] * second
    return jnp.concatenate([top, total, moment, one[3:4] + two[3:4], one[4:8]], axis=0)


def score_columns(unit, copies, whole, score, high, soft, perm_ref, group, steps, out_ref, out_sem, after):
    rows = unit.shape[0]
    step = 512
    per = len(copies) * step // whole.shape[0]
    for c in range(whole.shape[0] // step):
        for copy in copies[c * per : (c + 1) * per]:
            copy.wait()
        at = c * step
        chunk = score_scale * lax.dot_general(
            unit[...], whole[pl.ds(at, step)], (((1,), (1,)), ((), ())), preferred_element_type=f32
        )
        score[:, pl.ds(at, step)] = chunk
        peak = chunk[:, :128]
        for k in range(128, step, 128):
            peak = jnp.maximum(peak, chunk[:, k : k + 128])
        high[...] = peak if c == 0 else jnp.maximum(high[...], peak)

    places = column_places(group, steps)
    band = 128

    def one_band(at):
        here = pl.ds(at, band)
        perm = perm_ref[here, :]
        top = jnp.max(high[here, :], axis=1, keepdims=True)
        total = jnp.zeros((band, 128), f32)
        moment = jnp.zeros((band, 128), f32)
        found = jnp.zeros((band, 128), f32)
        for k in range(len(places)):
            cols = pl.ds(k * 128, 128)
            logit = score[here, cols]
            p = jnp.exp(logit - top)
            hit = perm == places[k]
            total += p
            moment += p * logit
            found += jnp.where(hit, logit, 0.0)
            soft[here, cols] = jnp.where(hit, 0.0, p).astype(bf16)
        if out_ref is not None:
            pltpu.make_async_copy(soft.at[here], out_ref.at[here], out_sem).start()
        sums = [jnp.sum(v, axis=1, keepdims=True) for v in (total, moment, found)]
        which = lax.broadcasted_iota(jnp.int32, (band, 128), 1)
        tile = jnp.where(which == 0, top, 0.0)
        for k, v in enumerate(sums):
            tile = jnp.where(which == k + 1, v, tile)
        high[here, :] = tile

    if after is None:
        pl.loop(0, rows // band)(lambda r: one_band(pl.multiple_of(r * band, band)))
    else:

        @pl.loop(0, rows // (2 * band))
        def _(r):
            for k in range(2):
                at = pl.multiple_of((2 * r + k) * band, band)
                one_band(at)
                after(at, band)

    return high[...]


def near_kernel(n, group, *refs):
    parts, perm_ref = refs[:8], refs[8]
    pieces = refs[9 : 9 + n]
    soft_ref, hard_ref, stats_ref, unit = refs[9 + n : 13 + n]
    whole, score, high, both, one_hot, soft, hard, sem, out_sem = refs[13 + n :]
    copies = fetch(pieces, whole, sem)
    rows, feats = parts[0].shape
    zh, core = lax.axis_index("zh"), lax.axis_index("core")
    square = jnp.zeros((rows, feats), f32)
    for ref in parts:
        part = ref[...].astype(f32)
        square += part * part
    rnorm = lax.rsqrt(jnp.sum(square, axis=1, keepdims=True) + epsilon)
    for k, ref in enumerate(parts):
        owner = lax.rem(zh + AROUND[k % 4], 4) * 2 + (core if k < 4 else 1 - core)
        to = pl.multiple_of(owner * feats, feats)
        unit[:, pl.ds(to, feats)] = (ref[...].astype(f32) * rnorm).astype(bf16)
    places = column_places(group, NEAR)

    def gradient(at, band):
        here = pl.ds(at, band)
        perm = perm_ref[here, :]
        for k in range(len(places)):
            one_hot[here, pl.ds(k * 128, 128)] = jnp.where(perm == places[k], 1.0, 0.0).astype(bf16)
        soft[here, :] = jnp.dot(both[here, :], whole[...], preferred_element_type=f32)
        hard[here, :] = jnp.dot(one_hot[here, :], whole[...], preferred_element_type=f32).astype(bf16)
        for k, (here_ref, there) in enumerate(((soft, soft_ref), (hard, hard_ref))):
            pltpu.make_async_copy(here_ref.at[here], there.at[here], out_sem.at[k]).start()

    tile = score_columns(
        unit, copies, whole, score, high, both, perm_ref, group, NEAR, None, None, gradient
    )
    which = lax.broadcasted_iota(jnp.int32, (rows, 128), 1)
    stats_ref[...] = jnp.where(which == 4, rnorm, tile).T[:8]
    pltpu.make_async_copy(soft, soft_ref, out_sem.at[0]).wait()
    pltpu.make_async_copy(hard, hard_ref, out_sem.at[1]).wait()


def far_score_kernel(n, group, *refs):
    unit, perm_ref, near_ref, sign_ref = refs[:4]
    pieces = refs[4 : 4 + n]
    out_ref, tops_ref, stats_ref = refs[4 + n : 7 + n]
    whole, score, high, soft, tops, sign, sem, out_sem, more_sem = refs[7 + n :]
    copies = fetch(pieces, whole, sem)
    flag = pltpu.make_async_copy(sign_ref, sign, more_sem)
    flag.start()
    lines = score_columns(
        unit, copies, whole, score, high, soft, perm_ref, group, FAR, out_ref, out_sem, None
    ).T[:8]
    near = near_ref[...]
    flag.wait()
    both = jnp.concatenate([merged(near, lines)[:5], sign[...], near[0:1], lines[0:1]], axis=0)
    tops[...] = both
    kept = pltpu.make_async_copy(tops, tops_ref, more_sem)
    kept.start()
    stats_ref[...] = both
    pltpu.make_async_copy(soft, out_ref, out_sem).wait()
    kept.wait()


def far_gradient_kernel(n, group, *refs):
    perm_ref, p_ref, tops_ref, near_soft_ref, near_hard_ref = refs[:5]
    pieces = refs[5 : 5 + n]
    soft_ref, hard_ref = refs[5 + n : 7 + n]
    whole, both, tops, soft, hard, sem, p_sem, more_sem, near_sem, out_sem = refs[7 + n :]
    copies = [
        pltpu.make_async_copy(p_ref, both.at[pl.ds(0, p_ref.shape[0])], p_sem),
        pltpu.make_async_copy(tops_ref, tops, more_sem),
    ]
    for copy in copies:
        copy.start()
    copies += fetch(pieces, whole, sem)
    copies += [
        pltpu.make_async_copy(near_soft_ref, soft, near_sem.at[0]),
        pltpu.make_async_copy(near_hard_ref, hard, near_sem.at[1]),
    ]
    copies[-2].start()
    copies[-1].start()
    rows = p_ref.shape[0]
    places = column_places(group, FAR)
    perm = perm_ref[...]
    for k in range(len(places)):
        both[pl.ds(rows, rows), pl.ds(k * 128, 128)] = jnp.where(
            perm == places[k], 1.0, 0.0
        ).astype(bf16)
    for copy in copies:
        copy.wait()
    top = tops[0:1]
    factors = as_columns([jnp.exp(tops[6:7] - top), jnp.exp(tops[7:8] - top)])
    first, second = factors[:, 0:1], factors[:, 1:2]
    step = 512
    for c in range(whole.shape[1] // step):
        cols = pl.ds(c * step, step)
        out = jnp.dot(both[...], whole[:, cols], preferred_element_type=f32)
        soft[:, cols] = first * soft[:, cols] + second * out[:rows]
        hard[:, cols] = hard[:, cols] + out[rows:].astype(bf16)
        for k, (here, there) in enumerate(((soft, soft_ref), (hard, hard_ref))):
            pltpu.make_async_copy(here.at[:, cols], there.at[:, cols], out_sem.at[k]).start()
    pltpu.make_async_copy(soft, soft_ref, out_sem.at[0]).wait()
    pltpu.make_async_copy(hard, hard_ref, out_sem.at[1]).wait()


def pair_kernel(mine_ref, theirs_ref, out_ref):
    even = lax.axis_index("core") == 0
    mine, theirs = mine_ref[...], theirs_ref[...]
    first, second = jnp.where(even, mine, theirs), jnp.where(even, theirs, mine)
    out_ref[...] = merged(first, second)


def combine_kernel(*refs):
    around, (tops_ref, soft_ref, hard_ref) = refs[:4], refs[4:7]
    keep_ref, give_ref, lines_ref = refs[7:10]
    every, tops, soft, hard, sem = refs[10:]
    copies = [
        pltpu.make_async_copy(tops_ref, tops, sem.at[2]),
        pltpu.make_async_copy(soft_ref, soft, sem.at[0]),
        pltpu.make_async_copy(hard_ref, hard, sem.at[1]),
    ]
    for copy in copies:
        copy.start()
    zh, core = lax.axis_index("zh"), lax.axis_index("core")
    feats = keep_ref.shape[2]
    for step, ref in zip(AROUND, around):
        every[lax.rem(zh + step, 4)] = ref[...]
    rest = [every[k] for k in range(4)]
    high = rest[0][0:1]
    for v in rest[1:]:
        high = jnp.maximum(high, v[0:1])
    mass = sum(jnp.exp(v[0:1] - high) * v[1:2] for v in rest)
    lse = high + jnp.log(mass)
    target = sum(v[3:4] for v in rest)
    mean = sum(jnp.exp(v[0:1] - lse) * v[2:3] for v in rest)
    copies[0].wait()
    sign = tops[5:6]
    lines_ref[0:1] = lse - target
    lines_ref[1:2] = sign * (mean - target)
    lines_ref[2:3] = tops[4:5]
    for_soft = score_scale * sign * jnp.exp(tops[0:1] - lse)
    weight = (sign * (jnp.exp(target - lse) - 1.0)).astype(bf16).astype(f32)
    cols = as_columns([for_soft, score_scale * weight])
    first, second = cols[:, 0:1], cols[:, 1:2]
    for copy in copies[1:]:
        copy.wait()
    for k, step in enumerate(AROUND):
        for out, which in ((keep_ref, core), (give_ref, 1 - core)):
            owner = lax.rem(zh + step, 4) * 2 + which
            at = pl.ds(pl.multiple_of(owner * feats, feats), feats)
            out[k] = first * soft[:, at] + second * hard[:, at].astype(f32)


def weight_kernel(images_ref, own_ref, one_ref, two_ref, three_ref, emb_ref, lines_ref, out_ref, held, sem):
    step = 1024
    copies = column_copies(images_ref, held, sem, step)
    grad_unit = own_ref[...]
    for ref in (one_ref, two_ref, three_ref):
        grad_unit += ref[...].astype(f32)
    cols = as_columns([lines_ref[1:2], lines_ref[2:3]])
    radial, rnorm = cols[:, 0:1], cols[:, 1:2]
    unit = emb_ref[...].astype(f32) * rnorm
    grad_emb = rnorm * (grad_unit - unit * radial)
    lines = grad_emb.T.astype(bf16)
    for k, copy in enumerate(copies):
        copy.wait()
        here = pl.ds(k * step, step)
        out_ref[here, :] = jnp.dot(lines, held[:, here], preferred_element_type=f32).T.astype(bf16)


def local(images, img_weight, texts, pair_perm, forget):
    rows, width = images.shape
    feats = img_weight.shape[1]
    group = texts.shape[0]

    copies = pl.pallas_call(
        spread_kernel,
        name="spread",
        out_shape=pltpu.HBM((16, *img_weight.shape), bf16),
        in_specs=[VMEM],
        out_specs=HBM,
        scratch_shapes=[pltpu.SemaphoreType.DMA((16,))],
        compiler_params=pltpu.CompilerParams(vmem_limit_bytes=2 << 20),
    )(img_weight)
    weight = exchanged(copies, PLANE).reshape(width, feats)
    other_texts = shifted(texts, "tw", 1)
    other_texts = pl.pallas_call(
        gate_kernel,
        name="gate",
        out_shape=jax.ShapeDtypeStruct(texts.shape, bf16),
        in_specs=[VMEM],
        out_specs=VMEM,
        compiler_params=pltpu.CompilerParams(vmem_limit_bytes=2 << 20),
    )(other_texts)
    signs = pl.pallas_call(
        sign_kernel,
        name="signs",
        out_shape=pltpu.HBM((1, rows), f32),
        in_specs=[VMEM],
        out_specs=HBM,
        scratch_shapes=[pltpu.VMEM((1, rows), f32), pltpu.SemaphoreType.DMA],
        compiler_params=pltpu.CompilerParams(vmem_limit_bytes=2 << 20),
    )(forget.reshape(1, rows))
    perm = pl.pallas_call(
        place_kernel,
        name="places",
        out_shape=jax.ShapeDtypeStruct((rows, 1), jnp.int32),
        in_specs=[VMEM],
        out_specs=VMEM,
        compiler_params=pltpu.CompilerParams(vmem_limit_bytes=2 << 20),
    )(pair_perm.reshape(1, rows))
    near, far = gathered_texts(texts, other_texts)
    n, m = len(near), len(far)
    near_rows, far_rows = (sum(q.shape[0] for q in group) for group in (near, far))
    embed = near[0].shape[1]

    emb = pl.pallas_call(
        embed_kernel,
        name="embed",
        out_shape=pltpu.HBM((rows, feats), bf16),
        in_specs=[HBM, VMEM],
        out_specs=HBM,
        scratch_shapes=[
            pltpu.VMEM((rows, width), bf16),
            pltpu.VMEM((rows, feats), bf16),
            pltpu.SemaphoreType.DMA((rows // 128,)),
            pltpu.SemaphoreType.DMA,
        ],
        compiler_params=pltpu.CompilerParams(vmem_limit_bytes=16 << 20),
        cost_estimate=pl.CostEstimate(
            flops=2 * rows * width * feats, bytes_accessed=7 << 20, transcendentals=0
        ),
    )(in_hbm(images), weight)
    mine = [emb, *from_others(emb, "zh")]
    theirs = [shifted(part, "core", 1) for part in mine]

    def cost(flops, columns):
        return pl.CostEstimate(
            flops=flops, bytes_accessed=4 * embed * columns, transcendentals=rows * columns
        )

    gradient_shape = (pltpu.HBM((rows, embed), f32), pltpu.HBM((rows, embed), bf16))
    gradient_scratch = [pltpu.VMEM((rows, embed), f32), pltpu.VMEM((rows, embed), bf16)]
    work = 2 * rows * embed
    near_soft, near_hard, near_stats, unit = pl.pallas_call(
        lambda *refs: near_kernel(n, group, *refs),
        name="near",
        out_shape=(
            *gradient_shape,
            jax.ShapeDtypeStruct((8, rows), f32),
            jax.ShapeDtypeStruct((rows, embed), bf16),
        ),
        in_specs=[*[VMEM] * 9, *[HBM] * n],
        out_specs=(HBM, HBM, VMEM, VMEM),
        scratch_shapes=[
            pltpu.VMEM((near_rows, embed), bf16),
            pltpu.VMEM((rows, near_rows), f32),
            pltpu.VMEM((rows, 128), f32),
            pltpu.VMEM((rows, near_rows), bf16),
            pltpu.VMEM((rows, near_rows), bf16),
            *gradient_scratch,
            pltpu.SemaphoreType.DMA((n,)),
            pltpu.SemaphoreType.DMA((2,)),
        ],
        compiler_params=pltpu.CompilerParams(vmem_limit_bytes=24 << 20),
        cost_estimate=cost(3 * work * near_rows, near_rows),
    )(*mine, *theirs, perm, *near)
    far_p, tops, stats = pl.pallas_call(
        lambda *refs: far_score_kernel(m, group, *refs),
        name="far_scores",
        out_shape=(
            pltpu.HBM((rows, far_rows), bf16),
            pltpu.HBM((8, rows), f32),
            jax.ShapeDtypeStruct((8, rows), f32),
        ),
        in_specs=[VMEM, VMEM, VMEM, HBM, *[HBM] * m],
        out_specs=(HBM, HBM, VMEM),
        scratch_shapes=[
            pltpu.VMEM((far_rows, embed), bf16),
            pltpu.VMEM((rows, far_rows), f32),
            pltpu.VMEM((rows, 128), f32),
            pltpu.VMEM((rows, far_rows), bf16),
            pltpu.VMEM((8, rows), f32),
            pltpu.VMEM((1, rows), f32),
            pltpu.SemaphoreType.DMA((m,)),
            pltpu.SemaphoreType.DMA,
            pltpu.SemaphoreType.DMA,
        ],
        compiler_params=pltpu.CompilerParams(vmem_limit_bytes=12 << 20),
        cost_estimate=cost(work * far_rows, far_rows),
    )(unit, perm, near_stats, in_hbm(signs), *far)
    swapped = shifted(stats, "core", 1)
    chip_stats = pl.pallas_call(
        pair_kernel,
        name="pair",
        out_shape=jax.ShapeDtypeStruct((8, rows), f32),
        in_specs=[VMEM, VMEM],
        out_specs=VMEM,
        compiler_params=pltpu.CompilerParams(vmem_limit_bytes=2 << 20),
    )(stats, swapped)
    every = [chip_stats, *from_others(chip_stats, "zh")]
    soft, hard = pl.pallas_call(
        lambda *refs: far_gradient_kernel(m, group, *refs),
        name="far_gradient",
        out_shape=gradient_shape,
        in_specs=[VMEM, HBM, HBM, HBM, HBM, *[HBM] * m],
        out_specs=(HBM, HBM),
        scratch_shapes=[
            pltpu.VMEM((far_rows, embed), bf16),
            pltpu.VMEM((2 * rows, far_rows), bf16),
            pltpu.VMEM((8, rows), f32),
            *gradient_scratch,
            pltpu.SemaphoreType.DMA((m,)),
            pltpu.SemaphoreType.DMA,
            pltpu.SemaphoreType.DMA,
            pltpu.SemaphoreType.DMA((2,)),
            pltpu.SemaphoreType.DMA((2,)),
        ],
        compiler_params=pltpu.CompilerParams(vmem_limit_bytes=16 << 20),
        cost_estimate=cost(2 * work * far_rows, far_rows),
    )(perm, in_hbm(far_p), in_hbm(tops), in_hbm(near_soft), in_hbm(near_hard), *far)

    keep, give, lines = pl.pallas_call(
        combine_kernel,
        name="combine",
        out_shape=(
            jax.ShapeDtypeStruct((4, rows, feats), f32),
            jax.ShapeDtypeStruct((4, rows, feats), f32),
            jax.ShapeDtypeStruct((8, rows), f32),
        ),
        in_specs=[VMEM, VMEM, VMEM, VMEM, HBM, HBM, HBM],
        out_specs=(VMEM, VMEM, VMEM),
        scratch_shapes=[
            pltpu.VMEM((4, 8, rows), f32),
            pltpu.VMEM((8, rows), f32),
            *gradient_scratch,
            pltpu.SemaphoreType.DMA((3,)),
        ],
        compiler_params=pltpu.CompilerParams(vmem_limit_bytes=20 << 20),
    )(*every, in_hbm(tops), in_hbm(soft), in_hbm(hard))

    pair_loss = lines[0]
    chip = keep + shifted(give, "core", 1)
    away = [chip[k].astype(bf16) for k in (2, 1, 3)]
    parts = [shifted(part, "zh", step) for part, step in zip(away, (1, -1, 2))]
    share = pl.pallas_call(
        weight_kernel,
        name="weight",
        out_shape=jax.ShapeDtypeStruct((width, feats), bf16),
        in_specs=[HBM, *[VMEM] * 6],
        out_specs=VMEM,
        scratch_shapes=[pltpu.VMEM((rows, width), bf16), pltpu.SemaphoreType.DMA((width // 1024,))],
        compiler_params=pltpu.CompilerParams(vmem_limit_bytes=16 << 20),
    )(in_hbm(images), chip[0], *parts, emb, lines)
    summed = jnp.sum(exchanged(share.reshape(16, -1, feats), PLANE).astype(f32), axis=0)
    weight_grad = summed + shifted(summed, "tw", 1)
    return (pair_loss, weight_grad)


def solution(mesh):
    finer = Mesh(mesh.devices.reshape(4, 4, 4, 2, mesh.shape["tower"]), AXES)
    return jax.shard_map(
        local,
        mesh=finer,
        in_specs=(
            P(FSDP_TOWER, None),
            P(PLANE, ("zh", "core")),
            P(("y", "x", "zh", "core", "tw"), None),
            P(FSDP_TOWER),
            P(FSDP_TOWER),
        ),
        out_specs=(P(FSDP_TOWER), P(PLANE, ("zh", "core"))),
        check_vma=False,
    )
```

```python
import jax
import jax.numpy as jnp
from jax import lax
from jax.experimental import pallas as pl
from jax.experimental.pallas import tpu as pltpu
from jax.sharding import Mesh
from jax.sharding import PartitionSpec as P

AXES = ("y", "x", "zh", "core", "tw")
PLANE = ("y", "x")
FSDP_TOWER = ("y", "x", "tw")
REL = (0, 3, 1, 2)
NEAR = ((0, 3), (0, 1))
AROUND = (0, 3, 1, 2)
FAR = ((1, 2), (3, 2))

epsilon = 1e-06
score_scale = 100.0
f32 = jnp.float32
bf16 = jnp.bfloat16
VMEM = pl.BlockSpec(memory_space=pltpu.VMEM)
HBM = pl.BlockSpec(memory_space=pltpu.HBM)


def shifted(x, axis, step):
    n = lax.axis_size(axis)
    return lax.ppermute(x, axis, [(i, (i + step) % n) for i in range(n)])


def in_hbm(x):
    return pltpu.with_memory_space_constraint(x, pltpu.HBM)


def exchanged(x, axis):
    return lax.all_to_all(x, axis, 0, 0, tiled=True)


def from_others(x, axis):
    return [shifted(x, axis, step) for step in (1, -1, 2)]


def gathered_texts(texts, other_texts):
    near, far = [], []
    for part, inner, outer in ((texts, "x", "y"), (other_texts, "y", "x")):
        below, above, across = (shifted(part, inner, step) for step in (1, -1, 2))
        halves = [jnp.concatenate([part, below]), jnp.concatenate([above, across])]
        for half, toward in zip(halves, (1, -1)):
            first = shifted(half, outer, toward)
            second = shifted(half, outer, -toward)
            across = shifted(first, outer, toward)
            near += [half, first]
            far += [second, across]
    return [in_hbm(piece) for piece in near], [in_hbm(piece) for piece in far]


def fetch(pieces, whole, sem):
    at, copies = 0, []
    for k, piece in enumerate(pieces):
        n = piece.shape[0]
        copies.append(pltpu.make_async_copy(piece, whole.at[pl.ds(at, n)], sem.at[k]))
        at += n
    for copy in copies:
        copy.start()
    return copies


def tp_index():
    return lax.axis_index("zh") * 2 + lax.axis_index("core")


def column_places(group, steps):
    y, x, tp, tower = lax.axis_index("y"), lax.axis_index("x"), tp_index(), lax.axis_index("tw")
    lane = lax.broadcasted_iota(jnp.int32, (1, 128), 1)
    places = []
    for side in range(2):
        tw = tower if side == 0 else 1 - tower
        for half in range(2):
            for step in steps[half]:
                firsts = []
                for inner in REL[2 * half : 2 * half + 2]:
                    ahead = (step, inner) if side == 0 else (inner, step)
                    plane = lax.rem(y + ahead[0], 4) * 4 + lax.rem(x + ahead[1], 4)
                    firsts.append(((plane * 8 + tp) * 2 + tw) * group)
                places.append(jnp.where(lane < group, firsts[0], firsts[1] - group) + lane)
    return places


def as_columns(lines):
    n = lines[0].shape[1]
    spare = jnp.zeros((128 - len(lines), n), f32)
    return jnp.concatenate([*lines, spare], axis=0).T


def column_copies(whole, held, sem, step):
    copies = []
    for k in range(whole.shape[1] // step):
        here = pl.ds(k * step, step)
        copies.append(pltpu.make_async_copy(whole.at[:, here], held.at[:, here], sem.at[k]))
        copies[-1].start()
    return copies


def gate_kernel(in_ref, out_ref):
    out_ref[...] = in_ref[...]


def spread_kernel(in_ref, out_ref):
    for k in range(out_ref.shape[0]):
        out_ref[k] = in_ref[...]


def sign_kernel(forget_ref, out_ref, sign, sem):
    sign[...] = 1.0 - 2.0 * forget_ref[...].astype(f32)
    copy = pltpu.make_async_copy(sign, out_ref, sem)
    copy.start()
    copy.wait()


def place_kernel(perm_ref, out_ref):
    out_ref[...] = as_columns([perm_ref[...].astype(f32)])[:, 0:1].astype(jnp.int32)


def embed_kernel(images_ref, weight_ref, out_ref, held, rounded, sem, out_sem):
    step = 128
    for k in range(images_ref.shape[0] // step):
        here = pl.ds(k * step, step)
        pltpu.make_async_copy(images_ref.at[here], held.at[here], sem.at[k]).start()

    @pl.loop(0, images_ref.shape[0] // step)
    def _(k):
        here = pl.ds(pl.multiple_of(k * step, step), step)
        pltpu.make_async_copy(images_ref.at[here], held.at[here], sem.at[k]).wait()
        rounded[here, :] = jnp.dot(
            held[here, :], weight_ref[...], preferred_element_type=f32
        ).astype(bf16)
        pltpu.make_async_copy(rounded.at[here], out_ref.at[here], out_sem).start()

    pltpu.make_async_copy(rounded, out_ref, out_sem).wait()


def merged(one, two):
    top = jnp.maximum(one[0:1], two[0:1])
    first, second = jnp.exp(one[0:1] - top), jnp.exp(two[0:1] - top)
    total = one[1:2] * first + two[1:2] * second
    moment = one[2:3] * first + two[2:3] * second
    return jnp.concatenate([top, total, moment, one[3:4] + two[3:4], one[4:8]], axis=0)


def score_columns(unit, copies, whole, score, high, soft, perm_ref, group, steps, out_ref, out_sem, after):
    rows = unit.shape[0]
    step = 512
    per = len(copies) * step // whole.shape[0]
    for c in range(whole.shape[0] // step):
        for copy in copies[c * per : (c + 1) * per]:
            copy.wait()
        at = c * step
        chunk = score_scale * lax.dot_general(
            unit[...], whole[pl.ds(at, step)], (((1,), (1,)), ((), ())), preferred_element_type=f32
        )
        score[:, pl.ds(at, step)] = chunk
        peak = chunk[:, :128]
        for k in range(128, step, 128):
            peak = jnp.maximum(peak, chunk[:, k : k + 128])
        high[...] = peak if c == 0 else jnp.maximum(high[...], peak)

    places = column_places(group, steps)
    band = 128

    def one_band(at):
        here = pl.ds(at, band)
        perm = perm_ref[here, :]
        top = jnp.max(high[here, :], axis=1, keepdims=True)
        total = jnp.zeros((band, 128), f32)
        moment = jnp.zeros((band, 128), f32)
        found = jnp.zeros((band, 128), f32)
        for k in range(len(places)):
            cols = pl.ds(k * 128, 128)
            logit = score[here, cols]
            p = jnp.exp(logit - top)
            hit = perm == places[k]
            total += p
            moment += p * logit
            found += jnp.where(hit, logit, 0.0)
            soft[here, cols] = jnp.where(hit, 0.0, p).astype(bf16)
        if out_ref is not None:
            pltpu.make_async_copy(soft.at[here], out_ref.at[here], out_sem).start()
        sums = [jnp.sum(v, axis=1, keepdims=True) for v in (total, moment, found)]
        which = lax.broadcasted_iota(jnp.int32, (band, 128), 1)
        tile = jnp.where(which == 0, top, 0.0)
        for k, v in enumerate(sums):
            tile = jnp.where(which == k + 1, v, tile)
        high[here, :] = tile

    if after is None:
        pl.loop(0, rows // band)(lambda r: one_band(pl.multiple_of(r * band, band)))
    else:

        @pl.loop(0, rows // (2 * band))
        def _(r):
            for k in range(2):
                at = pl.multiple_of((2 * r + k) * band, band)
                one_band(at)
                after(at, band)

    return high[...]


def near_kernel(n, group, *refs):
    parts, perm_ref = refs[:8], refs[8]
    pieces = refs[9 : 9 + n]
    soft_ref, hard_ref, stats_ref, unit = refs[9 + n : 13 + n]
    whole, score, high, both, one_hot, soft, hard, sem, out_sem = refs[13 + n :]
    copies = fetch(pieces, whole, sem)
    rows, feats = parts[0].shape
    zh, core = lax.axis_index("zh"), lax.axis_index("core")
    square = jnp.zeros((rows, feats), f32)
    for ref in parts:
        part = ref[...].astype(f32)
        square += part * part
    rnorm = lax.rsqrt(jnp.sum(square, axis=1, keepdims=True) + epsilon)
    for k, ref in enumerate(parts):
        owner = lax.rem(zh + AROUND[k % 4], 4) * 2 + (core if k < 4 else 1 - core)
        to = pl.multiple_of(owner * feats, feats)
        unit[:, pl.ds(to, feats)] = (ref[...].astype(f32) * rnorm).astype(bf16)
    places = column_places(group, NEAR)

    def gradient(at, band):
        here = pl.ds(at, band)
        perm = perm_ref[here, :]
        for k in range(len(places)):
            one_hot[here, pl.ds(k * 128, 128)] = jnp.where(perm == places[k], 1.0, 0.0).astype(bf16)
        soft[here, :] = jnp.dot(both[here, :], whole[...], preferred_element_type=f32)
        hard[here, :] = jnp.dot(one_hot[here, :], whole[...], preferred_element_type=f32).astype(bf16)
        for k, (here_ref, there) in enumerate(((soft, soft_ref), (hard, hard_ref))):
            pltpu.make_async_copy(here_ref.at[here], there.at[here], out_sem.at[k]).start()

    tile = score_columns(
        unit, copies, whole, score, high, both, perm_ref, group, NEAR, None, None, gradient
    )
    which = lax.broadcasted_iota(jnp.int32, (rows, 128), 1)
    stats_ref[...] = jnp.where(which == 4, rnorm, tile).T[:8]
    pltpu.make_async_copy(soft, soft_ref, out_sem.at[0]).wait()
    pltpu.make_async_copy(hard, hard_ref, out_sem.at[1]).wait()


def far_score_kernel(n, group, *refs):
    unit, perm_ref, near_ref, sign_ref = refs[:4]
    pieces = refs[4 : 4 + n]
    out_ref, tops_ref, stats_ref = refs[4 + n : 7 + n]
    whole, score, high, soft, tops, sign, sem, out_sem, more_sem = refs[7 + n :]
    copies = fetch(pieces, whole, sem)
    flag = pltpu.make_async_copy(sign_ref, sign, more_sem)
    flag.start()
    lines = score_columns(
        unit, copies, whole, score, high, soft, perm_ref, group, FAR, out_ref, out_sem, None
    ).T[:8]
    near = near_ref[...]
    flag.wait()
    both = jnp.concatenate([merged(near, lines)[:5], sign[...], near[0:1], lines[0:1]], axis=0)
    tops[...] = both
    kept = pltpu.make_async_copy(tops, tops_ref, more_sem)
    kept.start()
    stats_ref[...] = both
    pltpu.make_async_copy(soft, out_ref, out_sem).wait()
    kept.wait()


def far_gradient_kernel(n, group, *refs):
    perm_ref, p_ref, tops_ref, near_soft_ref, near_hard_ref = refs[:5]
    pieces = refs[5 : 5 + n]
    soft_ref, hard_ref = refs[5 + n : 7 + n]
    whole, both, tops, soft, hard, sem, p_sem, more_sem, near_sem, out_sem = refs[7 + n :]
    copies = [
        pltpu.make_async_copy(p_ref, both.at[pl.ds(0, p_ref.shape[0])], p_sem),
        pltpu.make_async_copy(tops_ref, tops, more_sem),
    ]
    for copy in copies:
        copy.start()
    copies += fetch(pieces, whole, sem)
    copies += [
        pltpu.make_async_copy(near_soft_ref, soft, near_sem.at[0]),
        pltpu.make_async_copy(near_hard_ref, hard, near_sem.at[1]),
    ]
    copies[-2].start()
    copies[-1].start()
    rows = p_ref.shape[0]
    places = column_places(group, FAR)
    perm = perm_ref[...]
    for k in range(len(places)):
        both[pl.ds(rows, rows), pl.ds(k * 128, 128)] = jnp.where(
            perm == places[k], 1.0, 0.0
        ).astype(bf16)
    for copy in copies:
        copy.wait()
    top = tops[0:1]
    factors = as_columns([jnp.exp(tops[6:7] - top), jnp.exp(tops[7:8] - top)])
    first, second = factors[:, 0:1], factors[:, 1:2]
    step = 512
    for c in range(whole.shape[1] // step):
        cols = pl.ds(c * step, step)
        out = jnp.dot(both[...], whole[:, cols], preferred_element_type=f32)
        soft[:, cols] = first * soft[:, cols] + second * out[:rows]
        hard[:, cols] = hard[:, cols] + out[rows:].astype(bf16)
        for k, (here, there) in enumerate(((soft, soft_ref), (hard, hard_ref))):
            pltpu.make_async_copy(here.at[:, cols], there.at[:, cols], out_sem.at[k]).start()
    pltpu.make_async_copy(soft, soft_ref, out_sem.at[0]).wait()
    pltpu.make_async_copy(hard, hard_ref, out_sem.at[1]).wait()


def pair_kernel(mine_ref, theirs_ref, out_ref):
    even = lax.axis_index("core") == 0
    mine, theirs = mine_ref[...], theirs_ref[...]
    first, second = jnp.where(even, mine, theirs), jnp.where(even, theirs, mine)
    out_ref[...] = merged(first, second)


def scaled_blocks(soft_ref, hard_ref, factors, out_ref, soft, hard, sem, which):
    zh = lax.axis_index("zh")
    feats = out_ref.shape[2]
    copies = []
    for k, step in enumerate(AROUND):
        owner = lax.rem(zh + step, 4) * 2 + which
        at = pl.ds(pl.multiple_of(owner * feats, feats), feats)
        copies.append(pltpu.make_async_copy(soft_ref.at[:, at], soft.at[k], sem.at[0, k]))
        copies.append(pltpu.make_async_copy(hard_ref.at[:, at], hard.at[k], sem.at[1, k]))
    for copy in copies:
        copy.start()
    cols = factors()
    first, second = cols[:, 0:1], cols[:, 1:2]
    for k in range(4):
        copies[2 * k].wait()
        copies[2 * k + 1].wait()
        out_ref[k] = first * soft[k] + second * hard[k].astype(f32)


def give_kernel(*refs):
    around, (tops_ref, soft_ref, hard_ref) = refs[:4], refs[4:7]
    give_ref, lines_ref = refs[7:9]
    every, tops, soft, hard, sem, tops_sem = refs[9:]
    copy = pltpu.make_async_copy(tops_ref, tops, tops_sem)
    copy.start()

    def factors():
        zh = lax.axis_index("zh")
        for step, ref in zip(AROUND, around):
            every[lax.rem(zh + step, 4)] = ref[...]
        rest = [every[k] for k in range(4)]
        high = rest[0][0:1]
        for v in rest[1:]:
            high = jnp.maximum(high, v[0:1])
        mass = sum(jnp.exp(v[0:1] - high) * v[1:2] for v in rest)
        lse = high + jnp.log(mass)
        target = sum(v[3:4] for v in rest)
        mean = sum(jnp.exp(v[0:1] - lse) * v[2:3] for v in rest)
        copy.wait()
        sign = tops[5:6]
        for_soft = score_scale * sign * jnp.exp(tops[0:1] - lse)
        weight = (sign * (jnp.exp(target - lse) - 1.0)).astype(bf16).astype(f32)
        lines_ref[0:1] = lse - target
        lines_ref[1:2] = sign * (mean - target)
        lines_ref[2:3] = tops[4:5]
        lines_ref[3:4] = for_soft
        lines_ref[4:5] = score_scale * weight
        return as_columns([for_soft, score_scale * weight])

    which = 1 - lax.axis_index("core")
    scaled_blocks(soft_ref, hard_ref, factors, give_ref, soft, hard, sem, which)


def keep_kernel(lines_ref, soft_ref, hard_ref, keep_ref, soft, hard, sem):
    def factors():
        return as_columns([lines_ref[3:4], lines_ref[4:5]])

    which = lax.axis_index("core")
    scaled_blocks(soft_ref, hard_ref, factors, keep_ref, soft, hard, sem, which)


def weight_kernel(images_ref, own_ref, one_ref, two_ref, three_ref, emb_ref, lines_ref, out_ref, held, sem):
    step = 1024
    copies = column_copies(images_ref, held, sem, step)
    grad_unit = own_ref[...]
    for ref in (one_ref, two_ref, three_ref):
        grad_unit += ref[...].astype(f32)
    cols = as_columns([lines_ref[1:2], lines_ref[2:3]])
    radial, rnorm = cols[:, 0:1], cols[:, 1:2]
    unit = emb_ref[...].astype(f32) * rnorm
    grad_emb = rnorm * (grad_unit - unit * radial)
    lines = grad_emb.T.astype(bf16)
    for k, copy in enumerate(copies):
        copy.wait()
        here = pl.ds(k * step, step)
        out_ref[here, :] = jnp.dot(lines, held[:, here], preferred_element_type=f32).T.astype(bf16)


def local(images, img_weight, texts, pair_perm, forget):
    rows, width = images.shape
    feats = img_weight.shape[1]
    group = texts.shape[0]

    copies = pl.pallas_call(
        spread_kernel,
        name="spread",
        out_shape=jax.ShapeDtypeStruct((16, *img_weight.shape), bf16),
        in_specs=[VMEM],
        out_specs=VMEM,
        compiler_params=pltpu.CompilerParams(vmem_limit_bytes=4 << 20),
    )(img_weight)
    weight = exchanged(copies, PLANE).reshape(width, feats)
    other_texts = shifted(texts, "tw", 1)
    other_texts = pl.pallas_call(
        gate_kernel,
        name="gate",
        out_shape=jax.ShapeDtypeStruct(texts.shape, bf16),
        in_specs=[VMEM],
        out_specs=VMEM,
        compiler_params=pltpu.CompilerParams(vmem_limit_bytes=2 << 20),
    )(other_texts)
    signs = pl.pallas_call(
        sign_kernel,
        name="signs",
        out_shape=pltpu.HBM((1, rows), f32),
        in_specs=[VMEM],
        out_specs=HBM,
        scratch_shapes=[pltpu.VMEM((1, rows), f32), pltpu.SemaphoreType.DMA],
        compiler_params=pltpu.CompilerParams(vmem_limit_bytes=2 << 20),
    )(forget.reshape(1, rows))
    perm = pl.pallas_call(
        place_kernel,
        name="places",
        out_shape=jax.ShapeDtypeStruct((rows, 1), jnp.int32),
        in_specs=[VMEM],
        out_specs=VMEM,
        compiler_params=pltpu.CompilerParams(vmem_limit_bytes=2 << 20),
    )(pair_perm.reshape(1, rows))
    near, far = gathered_texts(texts, other_texts)
    n, m = len(near), len(far)
    near_rows, far_rows = (sum(q.shape[0] for q in group) for group in (near, far))
    embed = near[0].shape[1]

    emb = pl.pallas_call(
        embed_kernel,
        name="embed",
        out_shape=pltpu.HBM((rows, feats), bf16),
        in_specs=[HBM, VMEM],
        out_specs=HBM,
        scratch_shapes=[
            pltpu.VMEM((rows, width), bf16),
            pltpu.VMEM((rows, feats), bf16),
            pltpu.SemaphoreType.DMA((rows // 128,)),
            pltpu.SemaphoreType.DMA,
        ],
        compiler_params=pltpu.CompilerParams(vmem_limit_bytes=16 << 20),
        cost_estimate=pl.CostEstimate(
            flops=2 * rows * width * feats, bytes_accessed=7 << 20, transcendentals=0
        ),
    )(in_hbm(images), weight)
    mine = [emb, *from_others(emb, "zh")]
    theirs = [shifted(part, "core", 1) for part in mine]

    def cost(flops, columns):
        return pl.CostEstimate(
            flops=flops, bytes_accessed=4 * embed * columns, transcendentals=rows * columns
        )

    gradient_shape = (pltpu.HBM((rows, embed), f32), pltpu.HBM((rows, embed), bf16))
    gradient_scratch = [pltpu.VMEM((rows, embed), f32), pltpu.VMEM((rows, embed), bf16)]
    work = 2 * rows * embed
    near_soft, near_hard, near_stats, unit = pl.pallas_call(
        lambda *refs: near_kernel(n, group, *refs),
        name="near",
        out_shape=(
            *gradient_shape,
            jax.ShapeDtypeStruct((8, rows), f32),
            jax.ShapeDtypeStruct((rows, embed), bf16),
        ),
        in_specs=[*[VMEM] * 9, *[HBM] * n],
        out_specs=(HBM, HBM, VMEM, VMEM),
        scratch_shapes=[
            pltpu.VMEM((near_rows, embed), bf16),
            pltpu.VMEM((rows, near_rows), f32),
            pltpu.VMEM((rows, 128), f32),
            pltpu.VMEM((rows, near_rows), bf16),
            pltpu.VMEM((rows, near_rows), bf16),
            *gradient_scratch,
            pltpu.SemaphoreType.DMA((n,)),
            pltpu.SemaphoreType.DMA((2,)),
        ],
        compiler_params=pltpu.CompilerParams(vmem_limit_bytes=24 << 20),
        cost_estimate=cost(3 * work * near_rows, near_rows),
    )(*mine, *theirs, perm, *near)
    far_p, tops, stats = pl.pallas_call(
        lambda *refs: far_score_kernel(m, group, *refs),
        name="far_scores",
        out_shape=(
            pltpu.HBM((rows, far_rows), bf16),
            pltpu.HBM((8, rows), f32),
            jax.ShapeDtypeStruct((8, rows), f32),
        ),
        in_specs=[VMEM, VMEM, VMEM, HBM, *[HBM] * m],
        out_specs=(HBM, HBM, VMEM),
        scratch_shapes=[
            pltpu.VMEM((far_rows, embed), bf16),
            pltpu.VMEM((rows, far_rows), f32),
            pltpu.VMEM((rows, 128), f32),
            pltpu.VMEM((rows, far_rows), bf16),
            pltpu.VMEM((8, rows), f32),
            pltpu.VMEM((1, rows), f32),
            pltpu.SemaphoreType.DMA((m,)),
            pltpu.SemaphoreType.DMA,
            pltpu.SemaphoreType.DMA,
        ],
        compiler_params=pltpu.CompilerParams(vmem_limit_bytes=12 << 20),
        cost_estimate=cost(work * far_rows, far_rows),
    )(unit, perm, near_stats, in_hbm(signs), *far)
    swapped = shifted(stats, "core", 1)
    chip_stats = pl.pallas_call(
        pair_kernel,
        name="pair",
        out_shape=jax.ShapeDtypeStruct((8, rows), f32),
        in_specs=[VMEM, VMEM],
        out_specs=VMEM,
        compiler_params=pltpu.CompilerParams(vmem_limit_bytes=2 << 20),
    )(stats, swapped)
    every = [chip_stats, *from_others(chip_stats, "zh")]
    soft, hard = pl.pallas_call(
        lambda *refs: far_gradient_kernel(m, group, *refs),
        name="far_gradient",
        out_shape=gradient_shape,
        in_specs=[VMEM, HBM, HBM, HBM, HBM, *[HBM] * m],
        out_specs=(HBM, HBM),
        scratch_shapes=[
            pltpu.VMEM((far_rows, embed), bf16),
            pltpu.VMEM((2 * rows, far_rows), bf16),
            pltpu.VMEM((8, rows), f32),
            *gradient_scratch,
            pltpu.SemaphoreType.DMA((m,)),
            pltpu.SemaphoreType.DMA,
            pltpu.SemaphoreType.DMA,
            pltpu.SemaphoreType.DMA((2,)),
            pltpu.SemaphoreType.DMA((2,)),
        ],
        compiler_params=pltpu.CompilerParams(vmem_limit_bytes=16 << 20),
        cost_estimate=cost(2 * work * far_rows, far_rows),
    )(perm, in_hbm(far_p), in_hbm(tops), in_hbm(near_soft), in_hbm(near_hard), *far)

    soft, hard = in_hbm(soft), in_hbm(hard)
    block_scratch = [
        pltpu.VMEM((4, rows, feats), f32),
        pltpu.VMEM((4, rows, feats), bf16),
        pltpu.SemaphoreType.DMA((2, 4)),
    ]
    give, lines = pl.pallas_call(
        give_kernel,
        name="give",
        out_shape=(
            jax.ShapeDtypeStruct((4, rows, feats), f32),
            jax.ShapeDtypeStruct((8, rows), f32),
        ),
        in_specs=[VMEM, VMEM, VMEM, VMEM, HBM, HBM, HBM],
        out_specs=(VMEM, VMEM),
        scratch_shapes=[
            pltpu.VMEM((4, 8, rows), f32),
            pltpu.VMEM((8, rows), f32),
            *block_scratch,
            pltpu.SemaphoreType.DMA,
        ],
        compiler_params=pltpu.CompilerParams(vmem_limit_bytes=12 << 20),
    )(*every, in_hbm(tops), soft, hard)
    given = shifted(give, "core", 1)
    keep = pl.pallas_call(
        keep_kernel,
        name="keep",
        out_shape=jax.ShapeDtypeStruct((4, rows, feats), f32),
        in_specs=[VMEM, HBM, HBM],
        out_specs=VMEM,
        scratch_shapes=block_scratch,
        compiler_params=pltpu.CompilerParams(vmem_limit_bytes=12 << 20),
    )(lines, soft, hard)

    pair_loss = lines[0]
    chip = keep + given
    away = [chip[k].astype(bf16) for k in (2, 1, 3)]
    parts = [shifted(part, "zh", step) for part, step in zip(away, (1, -1, 2))]
    share = pl.pallas_call(
        weight_kernel,
        name="weight",
        out_shape=jax.ShapeDtypeStruct((width, feats), bf16),
        in_specs=[HBM, *[VMEM] * 6],
        out_specs=VMEM,
        scratch_shapes=[pltpu.VMEM((rows, width), bf16), pltpu.SemaphoreType.DMA((width // 1024,))],
        compiler_params=pltpu.CompilerParams(vmem_limit_bytes=16 << 20),
    )(in_hbm(images), chip[0], *parts, emb, lines)
    summed = jnp.sum(exchanged(share.reshape(16, -1, feats), PLANE).astype(f32), axis=0)
    weight_grad = summed + shifted(summed, "tw", 1)
    return (pair_loss, weight_grad)


def solution(mesh):
    finer = Mesh(mesh.devices.reshape(4, 4, 4, 2, mesh.shape["tower"]), AXES)
    return jax.shard_map(
        local,
        mesh=finer,
        in_specs=(
            P(FSDP_TOWER, None),
            P(PLANE, ("zh", "core")),
            P(("y", "x", "zh", "core", "tw"), None),
            P(FSDP_TOWER),
            P(FSDP_TOWER),
        ),
        out_specs=(P(FSDP_TOWER), P(PLANE, ("zh", "core"))),
        check_vma=False,
    )
```

```python
import jax
import jax.numpy as jnp
from jax import lax
from jax.experimental import pallas as pl
from jax.experimental.pallas import tpu as pltpu
from jax.sharding import Mesh
from jax.sharding import PartitionSpec as P

AXES = ("y", "x", "zh", "core", "tw")
PLANE = ("y", "x")
FSDP_TOWER = ("y", "x", "tw")
REL = (0, 3, 1, 2)
NEAR = ((0, 3), (0, 1))
AROUND = (0, 3, 1, 2)
FAR = ((1, 2), (3, 2))

epsilon = 1e-06
score_scale = 100.0
f32 = jnp.float32
bf16 = jnp.bfloat16
VMEM = pl.BlockSpec(memory_space=pltpu.VMEM)
HBM = pl.BlockSpec(memory_space=pltpu.HBM)


def shifted(x, axis, step):
    n = lax.axis_size(axis)
    return lax.ppermute(x, axis, [(i, (i + step) % n) for i in range(n)])


def in_hbm(x):
    return pltpu.with_memory_space_constraint(x, pltpu.HBM)


def exchanged(x, axis):
    return lax.all_to_all(x, axis, 0, 0, tiled=True)


def from_others(x, axis):
    return [shifted(x, axis, step) for step in (1, -1, 2)]


def gathered_texts(texts, other_texts):
    near, far = [], []
    for part, inner, outer in ((texts, "x", "y"), (other_texts, "y", "x")):
        below, above, across = (shifted(part, inner, step) for step in (1, -1, 2))
        halves = [jnp.concatenate([part, below]), jnp.concatenate([above, across])]
        for half, toward in zip(halves, (1, -1)):
            first = shifted(half, outer, toward)
            second = shifted(half, outer, -toward)
            across = shifted(first, outer, toward)
            near += [half, first]
            far += [second, across]
    return [in_hbm(piece) for piece in near], [in_hbm(piece) for piece in far]


def fetch(pieces, whole, sem):
    at, copies = 0, []
    for k, piece in enumerate(pieces):
        n = piece.shape[0]
        copies.append(pltpu.make_async_copy(piece, whole.at[pl.ds(at, n)], sem.at[k]))
        at += n
    for copy in copies:
        copy.start()
    return copies


def tp_index():
    return lax.axis_index("zh") * 2 + lax.axis_index("core")


def column_places(group, steps):
    y, x, tp, tower = lax.axis_index("y"), lax.axis_index("x"), tp_index(), lax.axis_index("tw")
    lane = lax.broadcasted_iota(jnp.int32, (1, 128), 1)
    places = []
    for side in range(2):
        tw = tower if side == 0 else 1 - tower
        for half in range(2):
            for step in steps[half]:
                firsts = []
                for inner in REL[2 * half : 2 * half + 2]:
                    ahead = (step, inner) if side == 0 else (inner, step)
                    plane = lax.rem(y + ahead[0], 4) * 4 + lax.rem(x + ahead[1], 4)
                    firsts.append(((plane * 8 + tp) * 2 + tw) * group)
                places.append(jnp.where(lane < group, firsts[0], firsts[1] - group) + lane)
    return places


def as_columns(lines):
    n = lines[0].shape[1]
    spare = jnp.zeros((128 - len(lines), n), f32)
    return jnp.concatenate([*lines, spare], axis=0).T


def gate_kernel(in_ref, out_ref):
    out_ref[...] = in_ref[...]


def spread_kernel(in_ref, out_ref):
    for k in range(out_ref.shape[0]):
        out_ref[k] = in_ref[...]


def pull_kernel(in_ref, out_ref, sem):
    copy = pltpu.make_async_copy(in_ref, out_ref, sem)
    copy.start()
    copy.wait()


def pulled(x):
    return pl.pallas_call(
        pull_kernel,
        out_shape=pltpu.VMEM(x.shape, x.dtype),
        in_specs=[HBM],
        out_specs=VMEM,
        scratch_shapes=[pltpu.SemaphoreType.DMA],
        compiler_params=pltpu.CompilerParams(vmem_limit_bytes=2 << 20),
        cost_estimate=pl.CostEstimate(flops=0, bytes_accessed=2 * x.size * 2, transcendentals=0),
    )(in_hbm(x))


def sign_kernel(forget_ref, out_ref, sign, sem):
    sign[...] = 1.0 - 2.0 * forget_ref[...].astype(f32)
    copy = pltpu.make_async_copy(sign, out_ref, sem)
    copy.start()
    copy.wait()


def place_kernel(perm_ref, out_ref):
    out_ref[...] = as_columns([perm_ref[...].astype(f32)])[:, 0:1].astype(jnp.int32)


def embed_kernel(images_ref, weight_ref, out_ref, held, rounded, sem, out_sem):
    step = 128
    for k in range(images_ref.shape[0] // step):
        here = pl.ds(k * step, step)
        pltpu.make_async_copy(images_ref.at[here], held.at[here], sem.at[k]).start()

    @pl.loop(0, images_ref.shape[0] // step)
    def _(k):
        here = pl.ds(pl.multiple_of(k * step, step), step)
        pltpu.make_async_copy(images_ref.at[here], held.at[here], sem.at[k]).wait()
        rounded[here, :] = jnp.dot(
            held[here, :], weight_ref[...], preferred_element_type=f32
        ).astype(bf16)
        pltpu.make_async_copy(rounded.at[here], out_ref.at[here], out_sem).start()

    pltpu.make_async_copy(rounded, out_ref, out_sem).wait()


def merged(one, two):
    top = jnp.maximum(one[0:1], two[0:1])
    first, second = jnp.exp(one[0:1] - top), jnp.exp(two[0:1] - top)
    total = one[1:2] * first + two[1:2] * second
    moment = one[2:3] * first + two[2:3] * second
    return jnp.concatenate([top, total, moment, one[3:4] + two[3:4], one[4:8]], axis=0)


def score_columns(unit, copies, whole, score, high, soft, perm_ref, group, steps, out_ref, out_sem, after):
    rows = unit.shape[0]
    step = 512
    per = len(copies) * step // whole.shape[0]
    for c in range(whole.shape[0] // step):
        for copy in copies[c * per : (c + 1) * per]:
            copy.wait()
        at = c * step
        chunk = score_scale * lax.dot_general(
            unit[...], whole[pl.ds(at, step)], (((1,), (1,)), ((), ())), preferred_element_type=f32
        )
        score[:, pl.ds(at, step)] = chunk
        peak = chunk[:, :128]
        for k in range(128, step, 128):
            peak = jnp.maximum(peak, chunk[:, k : k + 128])
        high[...] = peak if c == 0 else jnp.maximum(high[...], peak)

    places = column_places(group, steps)
    band = 128

    def one_band(at):
        here = pl.ds(at, band)
        perm = perm_ref[here, :]
        top = jnp.max(high[here, :], axis=1, keepdims=True)
        total = jnp.zeros((band, 128), f32)
        moment = jnp.zeros((band, 128), f32)
        found = jnp.zeros((band, 128), f32)
        for k in range(len(places)):
            cols = pl.ds(k * 128, 128)
            logit = score[here, cols]
            p = jnp.exp(logit - top)
            hit = perm == places[k]
            total += p
            moment += p * logit
            found += jnp.where(hit, logit, 0.0)
            soft[here, cols] = jnp.where(hit, 0.0, p).astype(bf16)
        if out_ref is not None:
            pltpu.make_async_copy(soft.at[here], out_ref.at[here], out_sem).start()
        sums = [jnp.sum(v, axis=1, keepdims=True) for v in (total, moment, found)]
        which = lax.broadcasted_iota(jnp.int32, (band, 128), 1)
        tile = jnp.where(which == 0, top, 0.0)
        for k, v in enumerate(sums):
            tile = jnp.where(which == k + 1, v, tile)
        high[here, :] = tile

    if after is None:
        pl.loop(0, rows // band)(lambda r: one_band(pl.multiple_of(r * band, band)))
    else:

        @pl.loop(0, rows // (2 * band))
        def _(r):
            for k in range(2):
                at = pl.multiple_of((2 * r + k) * band, band)
                one_band(at)
                after(at, band)

    return high[...]


def near_kernel(n, group, *refs):
    parts, perm_ref = refs[:8], refs[8]
    pieces = refs[9 : 9 + n]
    soft_ref, hard_ref, stats_ref, unit = refs[9 + n : 13 + n]
    whole, score, high, both, one_hot, soft, hard, sem, out_sem = refs[13 + n :]
    copies = fetch(pieces, whole, sem)
    rows, feats = parts[0].shape
    zh, core = lax.axis_index("zh"), lax.axis_index("core")
    square = jnp.zeros((rows, feats), f32)
    for ref in parts:
        part = ref[...].astype(f32)
        square += part * part
    rnorm = lax.rsqrt(jnp.sum(square, axis=1, keepdims=True) + epsilon)
    for k, ref in enumerate(parts):
        owner = lax.rem(zh + AROUND[k % 4], 4) * 2 + (core if k < 4 else 1 - core)
        to = pl.multiple_of(owner * feats, feats)
        unit[:, pl.ds(to, feats)] = (ref[...].astype(f32) * rnorm).astype(bf16)
    places = column_places(group, NEAR)

    def gradient(at, band):
        here = pl.ds(at, band)
        perm = perm_ref[here, :]
        for k in range(len(places)):
            one_hot[here, pl.ds(k * 128, 128)] = jnp.where(perm == places[k], 1.0, 0.0).astype(bf16)
        soft[here, :] = jnp.dot(both[here, :], whole[...], preferred_element_type=f32)
        hard[here, :] = jnp.dot(one_hot[here, :], whole[...], preferred_element_type=f32).astype(bf16)
        for k, (here_ref, there) in enumerate(((soft, soft_ref), (hard, hard_ref))):
            pltpu.make_async_copy(here_ref.at[here], there.at[here], out_sem.at[k]).start()

    tile = score_columns(
        unit, copies, whole, score, high, both, perm_ref, group, NEAR, None, None, gradient
    )
    which = lax.broadcasted_iota(jnp.int32, (rows, 128), 1)
    stats_ref[...] = jnp.where(which == 4, rnorm, tile).T[:8]
    pltpu.make_async_copy(soft, soft_ref, out_sem.at[0]).wait()
    pltpu.make_async_copy(hard, hard_ref, out_sem.at[1]).wait()


def far_score_kernel(n, group, *refs):
    unit, perm_ref, near_ref, sign_ref = refs[:4]
    pieces = refs[4 : 4 + n]
    out_ref, tops_ref, stats_ref = refs[4 + n : 7 + n]
    whole, score, high, soft, tops, sign, sem, out_sem, more_sem = refs[7 + n :]
    copies = fetch(pieces, whole, sem)
    flag = pltpu.make_async_copy(sign_ref, sign, more_sem)
    flag.start()
    lines = score_columns(
        unit, copies, whole, score, high, soft, perm_ref, group, FAR, out_ref, out_sem, None
    ).T[:8]
    near = near_ref[...]
    flag.wait()
    both = jnp.concatenate([merged(near, lines)[:5], sign[...], near[0:1], lines[0:1]], axis=0)
    tops[...] = both
    kept = pltpu.make_async_copy(tops, tops_ref, more_sem)
    kept.start()
    stats_ref[...] = both
    pltpu.make_async_copy(soft, out_ref, out_sem).wait()
    kept.wait()


def far_gradient_kernel(n, group, *refs):
    perm_ref, p_ref, tops_ref, near_soft_ref, near_hard_ref = refs[:5]
    pieces = refs[5 : 5 + n]
    soft_ref, hard_ref = refs[5 + n : 7 + n]
    whole, both, tops, soft, hard, sem, p_sem, more_sem, near_sem, out_sem = refs[7 + n :]
    copies = [
        pltpu.make_async_copy(p_ref, both.at[pl.ds(0, p_ref.shape[0])], p_sem),
        pltpu.make_async_copy(tops_ref, tops, more_sem),
    ]
    for copy in copies:
        copy.start()
    copies += fetch(pieces, whole, sem)
    copies += [
        pltpu.make_async_copy(near_soft_ref, soft, near_sem.at[0]),
        pltpu.make_async_copy(near_hard_ref, hard, near_sem.at[1]),
    ]
    copies[-2].start()
    copies[-1].start()
    rows = p_ref.shape[0]
    places = column_places(group, FAR)
    perm = perm_ref[...]
    for k in range(len(places)):
        both[pl.ds(rows, rows), pl.ds(k * 128, 128)] = jnp.where(
            perm == places[k], 1.0, 0.0
        ).astype(bf16)
    for copy in copies:
        copy.wait()
    top = tops[0:1]
    factors = as_columns([jnp.exp(tops[6:7] - top), jnp.exp(tops[7:8] - top)])
    first, second = factors[:, 0:1], factors[:, 1:2]
    step = 512
    for c in range(whole.shape[1] // step):
        cols = pl.ds(c * step, step)
        out = jnp.dot(both[...], whole[:, cols], preferred_element_type=f32)
        soft[:, cols] = first * soft[:, cols] + second * out[:rows]
        hard[:, cols] = hard[:, cols] + out[rows:].astype(bf16)
        for k, (here, there) in enumerate(((soft, soft_ref), (hard, hard_ref))):
            pltpu.make_async_copy(here.at[:, cols], there.at[:, cols], out_sem.at[k]).start()
    pltpu.make_async_copy(soft, soft_ref, out_sem.at[0]).wait()
    pltpu.make_async_copy(hard, hard_ref, out_sem.at[1]).wait()


def pair_kernel(mine_ref, theirs_ref, out_ref):
    even = lax.axis_index("core") == 0
    mine, theirs = mine_ref[...], theirs_ref[...]
    first, second = jnp.where(even, mine, theirs), jnp.where(even, theirs, mine)
    out_ref[...] = merged(first, second)


def scaled_blocks(soft_ref, hard_ref, factors, out_ref, soft, hard, sem, which):
    zh = lax.axis_index("zh")
    feats = out_ref.shape[2]
    copies = []
    for k, step in enumerate(AROUND):
        owner = lax.rem(zh + step, 4) * 2 + which
        at = pl.ds(pl.multiple_of(owner * feats, feats), feats)
        copies.append(pltpu.make_async_copy(soft_ref.at[:, at], soft.at[k], sem.at[0, k]))
        copies.append(pltpu.make_async_copy(hard_ref.at[:, at], hard.at[k], sem.at[1, k]))
    for copy in copies:
        copy.start()
    cols = factors()
    first, second = cols[:, 0:1], cols[:, 1:2]
    for k in range(4):
        copies[2 * k].wait()
        copies[2 * k + 1].wait()
        out_ref[k] = first * soft[k] + second * hard[k].astype(f32)


def give_kernel(*refs):
    around, (tops_ref, soft_ref, hard_ref) = refs[:4], refs[4:7]
    give_ref, lines_ref = refs[7:9]
    every, tops, soft, hard, sem, tops_sem = refs[9:]
    copy = pltpu.make_async_copy(tops_ref, tops, tops_sem)
    copy.start()

    def factors():
        zh = lax.axis_index("zh")
        for step, ref in zip(AROUND, around):
            every[lax.rem(zh + step, 4)] = ref[...]
        rest = [every[k] for k in range(4)]
        high = rest[0][0:1]
        for v in rest[1:]:
            high = jnp.maximum(high, v[0:1])
        mass = sum(jnp.exp(v[0:1] - high) * v[1:2] for v in rest)
        lse = high + jnp.log(mass)
        target = sum(v[3:4] for v in rest)
        mean = sum(jnp.exp(v[0:1] - lse) * v[2:3] for v in rest)
        copy.wait()
        sign = tops[5:6]
        for_soft = score_scale * sign * jnp.exp(tops[0:1] - lse)
        weight = (sign * (jnp.exp(target - lse) - 1.0)).astype(bf16).astype(f32)
        lines_ref[0:1] = lse - target
        lines_ref[1:2] = sign * (mean - target)
        lines_ref[2:3] = tops[4:5]
        lines_ref[3:4] = for_soft
        lines_ref[4:5] = score_scale * weight
        return as_columns([for_soft, score_scale * weight])

    which = 1 - lax.axis_index("core")
    scaled_blocks(soft_ref, hard_ref, factors, give_ref, soft, hard, sem, which)


def keep_kernel(lines_ref, soft_ref, hard_ref, keep_ref, soft, hard, sem):
    def factors():
        return as_columns([lines_ref[3:4], lines_ref[4:5]])

    which = lax.axis_index("core")
    scaled_blocks(soft_ref, hard_ref, factors, keep_ref, soft, hard, sem, which)


def weight_kernel(images_ref, own_ref, one_ref, two_ref, three_ref, emb_ref, lines_ref, out_ref):
    step = 1024
    grad_unit = own_ref[...]
    for ref in (one_ref, two_ref, three_ref):
        grad_unit += ref[...].astype(f32)
    cols = as_columns([lines_ref[1:2], lines_ref[2:3]])
    radial, rnorm = cols[:, 0:1], cols[:, 1:2]
    unit = emb_ref[...].astype(f32) * rnorm
    grad_emb = rnorm * (grad_unit - unit * radial)
    lines = grad_emb.T.astype(bf16)
    for k in range(images_ref.shape[1] // step):
        here = pl.ds(k * step, step)
        out_ref[here, :] = jnp.dot(lines, images_ref[:, here], preferred_element_type=f32).T.astype(bf16)


def local(images, img_weight, texts, pair_perm, forget):
    rows, width = images.shape
    feats = img_weight.shape[1]
    group = texts.shape[0]

    copies = pl.pallas_call(
        spread_kernel,
        name="spread",
        out_shape=jax.ShapeDtypeStruct((16, *img_weight.shape), bf16),
        in_specs=[VMEM],
        out_specs=VMEM,
        compiler_params=pltpu.CompilerParams(vmem_limit_bytes=4 << 20),
    )(img_weight)
    weight = exchanged(copies, PLANE).reshape(width, feats)
    other_texts = shifted(texts, "tw", 1)
    other_texts = pl.pallas_call(
        gate_kernel,
        name="gate",
        out_shape=jax.ShapeDtypeStruct(texts.shape, bf16),
        in_specs=[VMEM],
        out_specs=VMEM,
        compiler_params=pltpu.CompilerParams(vmem_limit_bytes=2 << 20),
    )(other_texts)
    signs = pl.pallas_call(
        sign_kernel,
        name="signs",
        out_shape=pltpu.HBM((1, rows), f32),
        in_specs=[VMEM],
        out_specs=HBM,
        scratch_shapes=[pltpu.VMEM((1, rows), f32), pltpu.SemaphoreType.DMA],
        compiler_params=pltpu.CompilerParams(vmem_limit_bytes=2 << 20),
    )(forget.reshape(1, rows))
    perm = pl.pallas_call(
        place_kernel,
        name="places",
        out_shape=jax.ShapeDtypeStruct((rows, 1), jnp.int32),
        in_specs=[VMEM],
        out_specs=VMEM,
        compiler_params=pltpu.CompilerParams(vmem_limit_bytes=2 << 20),
    )(pair_perm.reshape(1, rows))
    near, far = gathered_texts(texts, other_texts)
    n, m = len(near), len(far)
    near_rows, far_rows = (sum(q.shape[0] for q in group) for group in (near, far))
    embed = near[0].shape[1]

    emb = pl.pallas_call(
        embed_kernel,
        name="embed",
        out_shape=pltpu.HBM((rows, feats), bf16),
        in_specs=[HBM, VMEM],
        out_specs=HBM,
        scratch_shapes=[
            pltpu.VMEM((rows, width), bf16),
            pltpu.VMEM((rows, feats), bf16),
            pltpu.SemaphoreType.DMA((rows // 128,)),
            pltpu.SemaphoreType.DMA,
        ],
        compiler_params=pltpu.CompilerParams(vmem_limit_bytes=16 << 20),
        cost_estimate=pl.CostEstimate(
            flops=2 * rows * width * feats, bytes_accessed=7 << 20, transcendentals=0
        ),
    )(in_hbm(images), weight)
    mine = [emb, *from_others(emb, "zh")]
    theirs = [shifted(part, "core", 1) for part in mine]

    def cost(flops, columns):
        return pl.CostEstimate(
            flops=flops, bytes_accessed=4 * embed * columns, transcendentals=rows * columns
        )

    gradient_shape = (pltpu.HBM((rows, embed), f32), pltpu.HBM((rows, embed), bf16))
    gradient_scratch = [pltpu.VMEM((rows, embed), f32), pltpu.VMEM((rows, embed), bf16)]
    work = 2 * rows * embed
    near_soft, near_hard, near_stats, unit = pl.pallas_call(
        lambda *refs: near_kernel(n, group, *refs),
        name="near",
        out_shape=(
            *gradient_shape,
            jax.ShapeDtypeStruct((8, rows), f32),
            jax.ShapeDtypeStruct((rows, embed), bf16),
        ),
        in_specs=[*[VMEM] * 9, *[HBM] * n],
        out_specs=(HBM, HBM, VMEM, VMEM),
        scratch_shapes=[
            pltpu.VMEM((near_rows, embed), bf16),
            pltpu.VMEM((rows, near_rows), f32),
            pltpu.VMEM((rows, 128), f32),
            pltpu.VMEM((rows, near_rows), bf16),
            pltpu.VMEM((rows, near_rows), bf16),
            *gradient_scratch,
            pltpu.SemaphoreType.DMA((n,)),
            pltpu.SemaphoreType.DMA((2,)),
        ],
        compiler_params=pltpu.CompilerParams(vmem_limit_bytes=24 << 20),
        cost_estimate=cost(3 * work * near_rows, near_rows),
    )(*mine, *theirs, perm, *near)
    far_p, tops, stats = pl.pallas_call(
        lambda *refs: far_score_kernel(m, group, *refs),
        name="far_scores",
        out_shape=(
            pltpu.HBM((rows, far_rows), bf16),
            pltpu.HBM((8, rows), f32),
            jax.ShapeDtypeStruct((8, rows), f32),
        ),
        in_specs=[VMEM, VMEM, VMEM, HBM, *[HBM] * m],
        out_specs=(HBM, HBM, VMEM),
        scratch_shapes=[
            pltpu.VMEM((far_rows, embed), bf16),
            pltpu.VMEM((rows, far_rows), f32),
            pltpu.VMEM((rows, 128), f32),
            pltpu.VMEM((rows, far_rows), bf16),
            pltpu.VMEM((8, rows), f32),
            pltpu.VMEM((1, rows), f32),
            pltpu.SemaphoreType.DMA((m,)),
            pltpu.SemaphoreType.DMA,
            pltpu.SemaphoreType.DMA,
        ],
        compiler_params=pltpu.CompilerParams(vmem_limit_bytes=12 << 20),
        cost_estimate=cost(work * far_rows, far_rows),
    )(unit, perm, near_stats, in_hbm(signs), *far)
    swapped = shifted(stats, "core", 1)
    chip_stats = pl.pallas_call(
        pair_kernel,
        name="pair",
        out_shape=jax.ShapeDtypeStruct((8, rows), f32),
        in_specs=[VMEM, VMEM],
        out_specs=VMEM,
        compiler_params=pltpu.CompilerParams(vmem_limit_bytes=2 << 20),
    )(stats, swapped)
    every = [chip_stats, *from_others(chip_stats, "zh")]
    soft, hard = pl.pallas_call(
        lambda *refs: far_gradient_kernel(m, group, *refs),
        name="far_gradient",
        out_shape=gradient_shape,
        in_specs=[VMEM, HBM, HBM, HBM, HBM, *[HBM] * m],
        out_specs=(HBM, HBM),
        scratch_shapes=[
            pltpu.VMEM((far_rows, embed), bf16),
            pltpu.VMEM((2 * rows, far_rows), bf16),
            pltpu.VMEM((8, rows), f32),
            *gradient_scratch,
            pltpu.SemaphoreType.DMA((m,)),
            pltpu.SemaphoreType.DMA,
            pltpu.SemaphoreType.DMA,
            pltpu.SemaphoreType.DMA((2,)),
            pltpu.SemaphoreType.DMA((2,)),
        ],
        compiler_params=pltpu.CompilerParams(vmem_limit_bytes=16 << 20),
        cost_estimate=cost(2 * work * far_rows, far_rows),
    )(perm, in_hbm(far_p), in_hbm(tops), in_hbm(near_soft), in_hbm(near_hard), *far)

    soft, hard = in_hbm(soft), in_hbm(hard)
    block_scratch = [
        pltpu.VMEM((4, rows, feats), f32),
        pltpu.VMEM((4, rows, feats), bf16),
        pltpu.SemaphoreType.DMA((2, 4)),
    ]
    give, lines = pl.pallas_call(
        give_kernel,
        name="give",
        out_shape=(
            jax.ShapeDtypeStruct((4, rows, feats), f32),
            jax.ShapeDtypeStruct((8, rows), f32),
        ),
        in_specs=[VMEM, VMEM, VMEM, VMEM, HBM, HBM, HBM],
        out_specs=(VMEM, VMEM),
        scratch_shapes=[
            pltpu.VMEM((4, 8, rows), f32),
            pltpu.VMEM((8, rows), f32),
            *block_scratch,
            pltpu.SemaphoreType.DMA,
        ],
        compiler_params=pltpu.CompilerParams(vmem_limit_bytes=12 << 20),
    )(*every, in_hbm(tops), soft, hard)
    given = shifted(give, "core", 1)
    keep = pl.pallas_call(
        keep_kernel,
        name="keep",
        out_shape=jax.ShapeDtypeStruct((4, rows, feats), f32),
        in_specs=[VMEM, HBM, HBM],
        out_specs=VMEM,
        scratch_shapes=block_scratch,
        compiler_params=pltpu.CompilerParams(vmem_limit_bytes=12 << 20),
    )(lines, soft, hard)

    pair_loss = lines[0]
    chip = keep + given
    away = [chip[k].astype(bf16) for k in (2, 1, 3)]
    parts = [shifted(part, "zh", step) for part, step in zip(away, (1, -1, 2))]
    share = pl.pallas_call(
        weight_kernel,
        name="weight",
        out_shape=jax.ShapeDtypeStruct((width, feats), bf16),
        in_specs=[VMEM] * 7,
        out_specs=VMEM,
        compiler_params=pltpu.CompilerParams(vmem_limit_bytes=8 << 20),
    )(pulled(images), chip[0], *parts, emb, lines)
    summed = jnp.sum(exchanged(share.reshape(16, -1, feats), PLANE).astype(f32), axis=0)
    weight_grad = summed + shifted(summed, "tw", 1)
    return (pair_loss, weight_grad)


def solution(mesh):
    finer = Mesh(mesh.devices.reshape(4, 4, 4, 2, mesh.shape["tower"]), AXES)
    return jax.shard_map(
        local,
        mesh=finer,
        in_specs=(
            P(FSDP_TOWER, None),
            P(PLANE, ("zh", "core")),
            P(("y", "x", "zh", "core", "tw"), None),
            P(FSDP_TOWER),
            P(FSDP_TOWER),
        ),
        out_specs=(P(FSDP_TOWER), P(PLANE, ("zh", "core"))),
        check_vma=False,
    )
```

```python
import jax
import jax.numpy as jnp
from jax import lax
from jax.experimental import pallas as pl
from jax.experimental.pallas import tpu as pltpu
from jax.sharding import Mesh
from jax.sharding import PartitionSpec as P

AXES = ("y", "x", "zh", "core", "tw")
PLANE = ("y", "x")
FSDP_TOWER = ("y", "x", "tw")
REL = (0, 3, 1, 2)
NEAR = ((0, 3), (0, 1))
AROUND = (0, 3, 1, 2)
FAR = ((1, 2), (3, 2))

epsilon = 1e-06
score_scale = 100.0
f32 = jnp.float32
bf16 = jnp.bfloat16
VMEM = pl.BlockSpec(memory_space=pltpu.VMEM)
HBM = pl.BlockSpec(memory_space=pltpu.HBM)


def shifted(x, axis, step):
    n = lax.axis_size(axis)
    return lax.ppermute(x, axis, [(i, (i + step) % n) for i in range(n)])


def in_hbm(x):
    return pltpu.with_memory_space_constraint(x, pltpu.HBM)


def exchanged(x, axis):
    return lax.all_to_all(x, axis, 0, 0, tiled=True)


def from_others(x, axis):
    return [shifted(x, axis, step) for step in (1, -1, 2)]


def gathered_texts(texts, other_texts):
    near, far = [], []
    for part, inner, outer in ((texts, "x", "y"), (other_texts, "y", "x")):
        below, above, across = (shifted(part, inner, step) for step in (1, -1, 2))
        halves = [jnp.concatenate([part, below]), jnp.concatenate([above, across])]
        for half, toward in zip(halves, (1, -1)):
            first = shifted(half, outer, toward)
            second = shifted(half, outer, -toward)
            across = shifted(first, outer, toward)
            near += [half, first]
            far += [second, across]
    return [in_hbm(piece) for piece in near], [in_hbm(piece) for piece in far]


def fetch(pieces, whole, sem):
    at, copies = 0, []
    for k, piece in enumerate(pieces):
        n = piece.shape[0]
        copies.append(pltpu.make_async_copy(piece, whole.at[pl.ds(at, n)], sem.at[k]))
        at += n
    for copy in copies:
        copy.start()
    return copies


def tp_index():
    return lax.axis_index("zh") * 2 + lax.axis_index("core")


def column_places(group, steps):
    y, x, tp, tower = lax.axis_index("y"), lax.axis_index("x"), tp_index(), lax.axis_index("tw")
    lane = lax.broadcasted_iota(jnp.int32, (1, 128), 1)
    places = []
    for side in range(2):
        tw = tower if side == 0 else 1 - tower
        for half in range(2):
            for step in steps[half]:
                firsts = []
                for inner in REL[2 * half : 2 * half + 2]:
                    ahead = (step, inner) if side == 0 else (inner, step)
                    plane = lax.rem(y + ahead[0], 4) * 4 + lax.rem(x + ahead[1], 4)
                    firsts.append(((plane * 8 + tp) * 2 + tw) * group)
                places.append(jnp.where(lane < group, firsts[0], firsts[1] - group) + lane)
    return places


def as_columns(lines):
    n = lines[0].shape[1]
    spare = jnp.zeros((128 - len(lines), n), f32)
    return jnp.concatenate([*lines, spare], axis=0).T


def gate_kernel(in_ref, out_ref):
    out_ref[...] = in_ref[...]


def spread_kernel(in_ref, out_ref, held, sem):
    copy = pltpu.make_async_copy(in_ref, held, sem)
    copy.start()
    copy.wait()
    for k in range(out_ref.shape[0]):
        out_ref[k] = held[...]


def pull_kernel(in_ref, out_ref, sem):
    copy = pltpu.make_async_copy(in_ref, out_ref, sem)
    copy.start()
    copy.wait()


def pulled(x):
    return pl.pallas_call(
        pull_kernel,
        out_shape=pltpu.VMEM(x.shape, x.dtype),
        in_specs=[HBM],
        out_specs=VMEM,
        scratch_shapes=[pltpu.SemaphoreType.DMA],
        compiler_params=pltpu.CompilerParams(vmem_limit_bytes=2 << 20),
        cost_estimate=pl.CostEstimate(flops=0, bytes_accessed=2 * x.size * 2, transcendentals=0),
    )(in_hbm(x))


def sign_kernel(forget_ref, out_ref, sign, sem):
    sign[...] = 1.0 - 2.0 * forget_ref[...].astype(f32)
    copy = pltpu.make_async_copy(sign, out_ref, sem)
    copy.start()
    copy.wait()


def place_kernel(perm_ref, out_ref):
    out_ref[...] = as_columns([perm_ref[...].astype(f32)])[:, 0:1].astype(jnp.int32)


def embed_kernel(images_ref, weight_ref, out_ref, held, rounded, sem, out_sem):
    step = 128
    for k in range(images_ref.shape[0] // step):
        here = pl.ds(k * step, step)
        pltpu.make_async_copy(images_ref.at[here], held.at[here], sem.at[k]).start()

    @pl.loop(0, images_ref.shape[0] // step)
    def _(k):
        here = pl.ds(pl.multiple_of(k * step, step), step)
        pltpu.make_async_copy(images_ref.at[here], held.at[here], sem.at[k]).wait()
        rounded[here, :] = jnp.dot(
            held[here, :], weight_ref[...], preferred_element_type=f32
        ).astype(bf16)
        pltpu.make_async_copy(rounded.at[here], out_ref.at[here], out_sem).start()

    pltpu.make_async_copy(rounded, out_ref, out_sem).wait()


def merged(one, two):
    top = jnp.maximum(one[0:1], two[0:1])
    first, second = jnp.exp(one[0:1] - top), jnp.exp(two[0:1] - top)
    total = one[1:2] * first + two[1:2] * second
    moment = one[2:3] * first + two[2:3] * second
    return jnp.concatenate([top, total, moment, one[3:4] + two[3:4], one[4:8]], axis=0)


def score_columns(unit, copies, whole, score, high, soft, perm_ref, group, steps, out_ref, out_sem, after):
    rows = unit.shape[0]
    step = 512
    per = len(copies) * step // whole.shape[0]
    for c in range(whole.shape[0] // step):
        for copy in copies[c * per : (c + 1) * per]:
            copy.wait()
        at = c * step
        chunk = score_scale * lax.dot_general(
            unit[...], whole[pl.ds(at, step)], (((1,), (1,)), ((), ())), preferred_element_type=f32
        )
        score[:, pl.ds(at, step)] = chunk
        peak = chunk[:, :128]
        for k in range(128, step, 128):
            peak = jnp.maximum(peak, chunk[:, k : k + 128])
        high[...] = peak if c == 0 else jnp.maximum(high[...], peak)

    places = column_places(group, steps)
    band = 128

    def one_band(at):
        here = pl.ds(at, band)
        perm = perm_ref[here, :]
        top = jnp.max(high[here, :], axis=1, keepdims=True)
        total = jnp.zeros((band, 128), f32)
        moment = jnp.zeros((band, 128), f32)
        found = jnp.zeros((band, 128), f32)
        for k in range(len(places)):
            cols = pl.ds(k * 128, 128)
            logit = score[here, cols]
            p = jnp.exp(logit - top)
            hit = perm == places[k]
            total += p
            moment += p * logit
            found += jnp.where(hit, logit, 0.0)
            soft[here, cols] = jnp.where(hit, 0.0, p).astype(bf16)
        if out_ref is not None:
            pltpu.make_async_copy(soft.at[here], out_ref.at[here], out_sem).start()
        sums = [jnp.sum(v, axis=1, keepdims=True) for v in (total, moment, found)]
        which = lax.broadcasted_iota(jnp.int32, (band, 128), 1)
        tile = jnp.where(which == 0, top, 0.0)
        for k, v in enumerate(sums):
            tile = jnp.where(which == k + 1, v, tile)
        high[here, :] = tile

    if after is None:
        pl.loop(0, rows // band)(lambda r: one_band(pl.multiple_of(r * band, band)))
    else:

        @pl.loop(0, rows // (2 * band))
        def _(r):
            for k in range(2):
                at = pl.multiple_of((2 * r + k) * band, band)
                one_band(at)
                after(at, band)

    return high[...]


def near_kernel(n, group, *refs):
    parts, perm_ref = refs[:8], refs[8]
    pieces = refs[9 : 9 + n]
    soft_ref, hard_ref, stats_ref, unit = refs[9 + n : 13 + n]
    whole, score, high, both, one_hot, soft, hard, sem, out_sem = refs[13 + n :]
    copies = fetch(pieces, whole, sem)
    rows, feats = parts[0].shape
    zh, core = lax.axis_index("zh"), lax.axis_index("core")
    square = jnp.zeros((rows, feats), f32)
    for ref in parts:
        part = ref[...].astype(f32)
        square += part * part
    rnorm = lax.rsqrt(jnp.sum(square, axis=1, keepdims=True) + epsilon)
    for k, ref in enumerate(parts):
        owner = lax.rem(zh + AROUND[k % 4], 4) * 2 + (core if k < 4 else 1 - core)
        to = pl.multiple_of(owner * feats, feats)
        unit[:, pl.ds(to, feats)] = (ref[...].astype(f32) * rnorm).astype(bf16)
    places = column_places(group, NEAR)

    def gradient(at, band):
        here = pl.ds(at, band)
        perm = perm_ref[here, :]
        for k in range(len(places)):
            one_hot[here, pl.ds(k * 128, 128)] = jnp.where(perm == places[k], 1.0, 0.0).astype(bf16)
        soft[here, :] = jnp.dot(both[here, :], whole[...], preferred_element_type=f32)
        hard[here, :] = jnp.dot(one_hot[here, :], whole[...], preferred_element_type=f32).astype(bf16)
        for k, (here_ref, there) in enumerate(((soft, soft_ref), (hard, hard_ref))):
            pltpu.make_async_copy(here_ref.at[here], there.at[here], out_sem.at[k]).start()

    tile = score_columns(
        unit, copies, whole, score, high, both, perm_ref, group, NEAR, None, None, gradient
    )
    which = lax.broadcasted_iota(jnp.int32, (rows, 128), 1)
    stats_ref[...] = jnp.where(which == 4, rnorm, tile).T[:8]
    pltpu.make_async_copy(soft, soft_ref, out_sem.at[0]).wait()
    pltpu.make_async_copy(hard, hard_ref, out_sem.at[1]).wait()


def far_score_kernel(n, group, *refs):
    unit, perm_ref, near_ref, sign_ref = refs[:4]
    pieces = refs[4 : 4 + n]
    out_ref, tops_ref, stats_ref = refs[4 + n : 7 + n]
    whole, score, high, soft, tops, sign, sem, out_sem, more_sem = refs[7 + n :]
    copies = fetch(pieces, whole, sem)
    flag = pltpu.make_async_copy(sign_ref, sign, more_sem)
    flag.start()
    lines = score_columns(
        unit, copies, whole, score, high, soft, perm_ref, group, FAR, out_ref, out_sem, None
    ).T[:8]
    near = near_ref[...]
    flag.wait()
    both = jnp.concatenate([merged(near, lines)[:5], sign[...], near[0:1], lines[0:1]], axis=0)
    tops[...] = both
    kept = pltpu.make_async_copy(tops, tops_ref, more_sem)
    kept.start()
    stats_ref[...] = both
    pltpu.make_async_copy(soft, out_ref, out_sem).wait()
    kept.wait()


def far_gradient_kernel(n, group, *refs):
    perm_ref, p_ref, tops_ref, near_soft_ref, near_hard_ref = refs[:5]
    pieces = refs[5 : 5 + n]
    soft_ref, hard_ref = refs[5 + n : 7 + n]
    whole, both, tops, soft, hard, sem, p_sem, more_sem, near_sem, out_sem = refs[7 + n :]
    copies = [
        pltpu.make_async_copy(p_ref, both.at[pl.ds(0, p_ref.shape[0])], p_sem),
        pltpu.make_async_copy(tops_ref, tops, more_sem),
    ]
    for copy in copies:
        copy.start()
    copies += fetch(pieces, whole, sem)
    copies += [
        pltpu.make_async_copy(near_soft_ref, soft, near_sem.at[0]),
        pltpu.make_async_copy(near_hard_ref, hard, near_sem.at[1]),
    ]
    copies[-2].start()
    copies[-1].start()
    rows = p_ref.shape[0]
    places = column_places(group, FAR)
    perm = perm_ref[...]
    for k in range(len(places)):
        both[pl.ds(rows, rows), pl.ds(k * 128, 128)] = jnp.where(
            perm == places[k], 1.0, 0.0
        ).astype(bf16)
    for copy in copies:
        copy.wait()
    top = tops[0:1]
    factors = as_columns([jnp.exp(tops[6:7] - top), jnp.exp(tops[7:8] - top)])
    first, second = factors[:, 0:1], factors[:, 1:2]
    step = 512
    for c in range(whole.shape[1] // step):
        cols = pl.ds(c * step, step)
        out = jnp.dot(both[...], whole[:, cols], preferred_element_type=f32)
        soft[:, cols] = first * soft[:, cols] + second * out[:rows]
        hard[:, cols] = hard[:, cols] + out[rows:].astype(bf16)
        for k, (here, there) in enumerate(((soft, soft_ref), (hard, hard_ref))):
            pltpu.make_async_copy(here.at[:, cols], there.at[:, cols], out_sem.at[k]).start()
    pltpu.make_async_copy(soft, soft_ref, out_sem.at[0]).wait()
    pltpu.make_async_copy(hard, hard_ref, out_sem.at[1]).wait()


def pair_kernel(mine_ref, theirs_ref, out_ref):
    even = lax.axis_index("core") == 0
    mine, theirs = mine_ref[...], theirs_ref[...]
    first, second = jnp.where(even, mine, theirs), jnp.where(even, theirs, mine)
    out_ref[...] = merged(first, second)


def scaled_blocks(soft_ref, hard_ref, factors, out_ref, soft, hard, sem, which):
    zh = lax.axis_index("zh")
    feats = out_ref.shape[2]
    copies = []
    for k, step in enumerate(AROUND):
        owner = lax.rem(zh + step, 4) * 2 + which
        at = pl.ds(pl.multiple_of(owner * feats, feats), feats)
        copies.append(pltpu.make_async_copy(soft_ref.at[:, at], soft.at[k], sem.at[0, k]))
        copies.append(pltpu.make_async_copy(hard_ref.at[:, at], hard.at[k], sem.at[1, k]))
    for copy in copies:
        copy.start()
    cols = factors()
    first, second = cols[:, 0:1], cols[:, 1:2]
    for k in range(4):
        copies[2 * k].wait()
        copies[2 * k + 1].wait()
        out_ref[k] = first * soft[k] + second * hard[k].astype(f32)


def give_kernel(*refs):
    around, (tops_ref, soft_ref, hard_ref) = refs[:4], refs[4:7]
    give_ref, lines_ref = refs[7:9]
    every, tops, soft, hard, sem, tops_sem = refs[9:]
    copy = pltpu.make_async_copy(tops_ref, tops, tops_sem)
    copy.start()

    def factors():
        zh = lax.axis_index("zh")
        for step, ref in zip(AROUND, around):
            every[lax.rem(zh + step, 4)] = ref[...]
        rest = [every[k] for k in range(4)]
        high = rest[0][0:1]
        for v in rest[1:]:
            high = jnp.maximum(high, v[0:1])
        mass = sum(jnp.exp(v[0:1] - high) * v[1:2] for v in rest)
        lse = high + jnp.log(mass)
        target = sum(v[3:4] for v in rest)
        mean = sum(jnp.exp(v[0:1] - lse) * v[2:3] for v in rest)
        copy.wait()
        sign = tops[5:6]
        for_soft = score_scale * sign * jnp.exp(tops[0:1] - lse)
        weight = (sign * (jnp.exp(target - lse) - 1.0)).astype(bf16).astype(f32)
        lines_ref[0:1] = lse - target
        lines_ref[1:2] = sign * (mean - target)
        lines_ref[2:3] = tops[4:5]
        lines_ref[3:4] = for_soft
        lines_ref[4:5] = score_scale * weight
        return as_columns([for_soft, score_scale * weight])

    which = 1 - lax.axis_index("core")
    scaled_blocks(soft_ref, hard_ref, factors, give_ref, soft, hard, sem, which)


def keep_kernel(lines_ref, soft_ref, hard_ref, keep_ref, soft, hard, sem):
    def factors():
        return as_columns([lines_ref[3:4], lines_ref[4:5]])

    which = lax.axis_index("core")
    scaled_blocks(soft_ref, hard_ref, factors, keep_ref, soft, hard, sem, which)


def weight_kernel(images_ref, own_ref, one_ref, two_ref, three_ref, emb_ref, lines_ref, out_ref):
    step = 1024
    grad_unit = own_ref[...]
    for ref in (one_ref, two_ref, three_ref):
        grad_unit += ref[...].astype(f32)
    cols = as_columns([lines_ref[1:2], lines_ref[2:3]])
    radial, rnorm = cols[:, 0:1], cols[:, 1:2]
    unit = emb_ref[...].astype(f32) * rnorm
    grad_emb = rnorm * (grad_unit - unit * radial)
    lines = grad_emb.T.astype(bf16)
    for k in range(images_ref.shape[1] // step):
        here = pl.ds(k * step, step)
        out_ref[here, :] = jnp.dot(lines, images_ref[:, here], preferred_element_type=f32).T.astype(bf16)


def local(images, img_weight, texts, pair_perm, forget):
    rows, width = images.shape
    feats = img_weight.shape[1]
    group = texts.shape[0]

    copies = pl.pallas_call(
        spread_kernel,
        name="spread",
        out_shape=jax.ShapeDtypeStruct((16, *img_weight.shape), bf16),
        in_specs=[HBM],
        out_specs=VMEM,
        scratch_shapes=[
            pltpu.VMEM(img_weight.shape, bf16),
            pltpu.SemaphoreType.DMA,
        ],
        compiler_params=pltpu.CompilerParams(vmem_limit_bytes=4 << 20),
    )(in_hbm(img_weight))
    weight = exchanged(copies, PLANE).reshape(width, feats)
    other_texts = shifted(texts, "tw", 1)
    other_texts = pl.pallas_call(
        gate_kernel,
        name="gate",
        out_shape=jax.ShapeDtypeStruct(texts.shape, bf16),
        in_specs=[VMEM],
        out_specs=VMEM,
        compiler_params=pltpu.CompilerParams(vmem_limit_bytes=2 << 20),
    )(other_texts)
    signs = pl.pallas_call(
        sign_kernel,
        name="signs",
        out_shape=pltpu.HBM((1, rows), f32),
        in_specs=[VMEM],
        out_specs=HBM,
        scratch_shapes=[pltpu.VMEM((1, rows), f32), pltpu.SemaphoreType.DMA],
        compiler_params=pltpu.CompilerParams(vmem_limit_bytes=2 << 20),
    )(forget.reshape(1, rows))
    perm = pl.pallas_call(
        place_kernel,
        name="places",
        out_shape=jax.ShapeDtypeStruct((rows, 1), jnp.int32),
        in_specs=[VMEM],
        out_specs=VMEM,
        compiler_params=pltpu.CompilerParams(vmem_limit_bytes=2 << 20),
    )(pair_perm.reshape(1, rows))
    near, far = gathered_texts(texts, other_texts)
    n, m = len(near), len(far)
    near_rows, far_rows = (sum(q.shape[0] for q in group) for group in (near, far))
    embed = near[0].shape[1]

    emb = pl.pallas_call(
        embed_kernel,
        name="embed",
        out_shape=pltpu.HBM((rows, feats), bf16),
        in_specs=[HBM, VMEM],
        out_specs=HBM,
        scratch_shapes=[
            pltpu.VMEM((rows, width), bf16),
            pltpu.VMEM((rows, feats), bf16),
            pltpu.SemaphoreType.DMA((rows // 128,)),
            pltpu.SemaphoreType.DMA,
        ],
        compiler_params=pltpu.CompilerParams(vmem_limit_bytes=16 << 20),
        cost_estimate=pl.CostEstimate(
            flops=2 * rows * width * feats, bytes_accessed=7 << 20, transcendentals=0
        ),
    )(in_hbm(images), weight)
    mine = [emb, *from_others(emb, "zh")]
    theirs = [shifted(part, "core", 1) for part in mine]

    def cost(flops, columns):
        return pl.CostEstimate(
            flops=flops, bytes_accessed=4 * embed * columns, transcendentals=rows * columns
        )

    gradient_shape = (pltpu.HBM((rows, embed), f32), pltpu.HBM((rows, embed), bf16))
    gradient_scratch = [pltpu.VMEM((rows, embed), f32), pltpu.VMEM((rows, embed), bf16)]
    work = 2 * rows * embed
    near_soft, near_hard, near_stats, unit = pl.pallas_call(
        lambda *refs: near_kernel(n, group, *refs),
        name="near",
        out_shape=(
            *gradient_shape,
            jax.ShapeDtypeStruct((8, rows), f32),
            jax.ShapeDtypeStruct((rows, embed), bf16),
        ),
        in_specs=[*[VMEM] * 9, *[HBM] * n],
        out_specs=(HBM, HBM, VMEM, VMEM),
        scratch_shapes=[
            pltpu.VMEM((near_rows, embed), bf16),
            pltpu.VMEM((rows, near_rows), f32),
            pltpu.VMEM((rows, 128), f32),
            pltpu.VMEM((rows, near_rows), bf16),
            pltpu.VMEM((rows, near_rows), bf16),
            *gradient_scratch,
            pltpu.SemaphoreType.DMA((n,)),
            pltpu.SemaphoreType.DMA((2,)),
        ],
        compiler_params=pltpu.CompilerParams(vmem_limit_bytes=24 << 20),
        cost_estimate=cost(3 * work * near_rows, near_rows),
    )(*mine, *theirs, perm, *near)
    far_p, tops, stats = pl.pallas_call(
        lambda *refs: far_score_kernel(m, group, *refs),
        name="far_scores",
        out_shape=(
            pltpu.HBM((rows, far_rows), bf16),
            pltpu.HBM((8, rows), f32),
            jax.ShapeDtypeStruct((8, rows), f32),
        ),
        in_specs=[VMEM, VMEM, VMEM, HBM, *[HBM] * m],
        out_specs=(HBM, HBM, VMEM),
        scratch_shapes=[
            pltpu.VMEM((far_rows, embed), bf16),
            pltpu.VMEM((rows, far_rows), f32),
            pltpu.VMEM((rows, 128), f32),
            pltpu.VMEM((rows, far_rows), bf16),
            pltpu.VMEM((8, rows), f32),
            pltpu.VMEM((1, rows), f32),
            pltpu.SemaphoreType.DMA((m,)),
            pltpu.SemaphoreType.DMA,
            pltpu.SemaphoreType.DMA,
        ],
        compiler_params=pltpu.CompilerParams(vmem_limit_bytes=12 << 20),
        cost_estimate=cost(work * far_rows, far_rows),
    )(unit, perm, near_stats, in_hbm(signs), *far)
    swapped = shifted(stats, "core", 1)
    chip_stats = pl.pallas_call(
        pair_kernel,
        name="pair",
        out_shape=jax.ShapeDtypeStruct((8, rows), f32),
        in_specs=[VMEM, VMEM],
        out_specs=VMEM,
        compiler_params=pltpu.CompilerParams(vmem_limit_bytes=2 << 20),
    )(stats, swapped)
    every = [chip_stats, *from_others(chip_stats, "zh")]
    soft, hard = pl.pallas_call(
        lambda *refs: far_gradient_kernel(m, group, *refs),
        name="far_gradient",
        out_shape=gradient_shape,
        in_specs=[VMEM, HBM, HBM, HBM, HBM, *[HBM] * m],
        out_specs=(HBM, HBM),
        scratch_shapes=[
            pltpu.VMEM((far_rows, embed), bf16),
            pltpu.VMEM((2 * rows, far_rows), bf16),
            pltpu.VMEM((8, rows), f32),
            *gradient_scratch,
            pltpu.SemaphoreType.DMA((m,)),
            pltpu.SemaphoreType.DMA,
            pltpu.SemaphoreType.DMA,
            pltpu.SemaphoreType.DMA((2,)),
            pltpu.SemaphoreType.DMA((2,)),
        ],
        compiler_params=pltpu.CompilerParams(vmem_limit_bytes=16 << 20),
        cost_estimate=cost(2 * work * far_rows, far_rows),
    )(perm, in_hbm(far_p), in_hbm(tops), in_hbm(near_soft), in_hbm(near_hard), *far)

    soft, hard = in_hbm(soft), in_hbm(hard)
    block_scratch = [
        pltpu.VMEM((4, rows, feats), f32),
        pltpu.VMEM((4, rows, feats), bf16),
        pltpu.SemaphoreType.DMA((2, 4)),
    ]
    give, lines = pl.pallas_call(
        give_kernel,
        name="give",
        out_shape=(
            jax.ShapeDtypeStruct((4, rows, feats), f32),
            jax.ShapeDtypeStruct((8, rows), f32),
        ),
        in_specs=[VMEM, VMEM, VMEM, VMEM, HBM, HBM, HBM],
        out_specs=(VMEM, VMEM),
        scratch_shapes=[
            pltpu.VMEM((4, 8, rows), f32),
            pltpu.VMEM((8, rows), f32),
            *block_scratch,
            pltpu.SemaphoreType.DMA,
        ],
        compiler_params=pltpu.CompilerParams(vmem_limit_bytes=12 << 20),
    )(*every, in_hbm(tops), soft, hard)
    given = shifted(give, "core", 1)
    keep = pl.pallas_call(
        keep_kernel,
        name="keep",
        out_shape=jax.ShapeDtypeStruct((4, rows, feats), f32),
        in_specs=[VMEM, HBM, HBM],
        out_specs=VMEM,
        scratch_shapes=block_scratch,
        compiler_params=pltpu.CompilerParams(vmem_limit_bytes=12 << 20),
    )(lines, soft, hard)

    pair_loss = lines[0]
    chip = keep + given
    away = [chip[k].astype(bf16) for k in (2, 1, 3)]
    parts = [shifted(part, "zh", step) for part, step in zip(away, (1, -1, 2))]
    share = pl.pallas_call(
        weight_kernel,
        name="weight",
        out_shape=jax.ShapeDtypeStruct((width, feats), bf16),
        in_specs=[VMEM] * 7,
        out_specs=VMEM,
        compiler_params=pltpu.CompilerParams(vmem_limit_bytes=8 << 20),
    )(pulled(images), chip[0], *parts, emb, lines)
    summed = jnp.sum(exchanged(share.reshape(16, -1, feats), PLANE).astype(f32), axis=0)
    weight_grad = summed + shifted(summed, "tw", 1)
    return (pair_loss, weight_grad)


def solution(mesh):
    finer = Mesh(mesh.devices.reshape(4, 4, 4, 2, mesh.shape["tower"]), AXES)
    return jax.shard_map(
        local,
        mesh=finer,
        in_specs=(
            P(FSDP_TOWER, None),
            P(PLANE, ("zh", "core")),
            P(("y", "x", "zh", "core", "tw"), None),
            P(FSDP_TOWER),
            P(FSDP_TOWER),
        ),
        out_specs=(P(FSDP_TOWER), P(PLANE, ("zh", "core"))),
        check_vma=False,
    )
```
